128 devices in a mesh: sym: 8 (over y, x_lo), row: 16 (over x_hi, z, core).
Axes of the slice: x: 4 (x_hi: 2, x_lo: 2; x = x_hi * 2 + x_lo), y: 4, z: 4, core: 2. Of those that a mesh axis runs over, the one named last changes fastest.
Arguments:
- inner_state: float32 [8, 6144, 128], P('sym', 'row'), may hold values from -6 to 6
- outer_state: float32 [8, 24, 128, 2048], P('sym', None, None, 'row'), may hold values from -6 to 6
- block_hamiltonian: bfloat16 [8, 6144, 6144], P('sym', 'row'), may hold values from -2 to 2, as said below
- dipole: bfloat16 [8, 6144, 6144], P('sym', 'row'), may hold values from -0.078125 to 0.078125
- field_strength: float32 [64], replicated, may hold values from -1.2 to 1.2
- dipole_links: int32 [7, 64], replicated, may hold values 0 or 1
- ghost_amplitude: float32 [8, 2, 6144], P('sym'), may hold values from -0.4 to 0.4
- surface_amplitude: float32 [8, 6144], P('sym'), may hold values from -3 to 3
- state_channel: int32 [8, 6144], P('sym'), may hold values from 0 to 23
- threshold: float32 [8, 24], P('sym'), may hold values from 0 to 1
Outputs:
- inner_next: float32 [8, 6144, 128], P('sym', 'row')
- outer_next: float32 [8, 24, 128, 2048], P('sym', None, None, 'row')
The draws below stay inside these ranges and needn't reach their ends.
Inputs may be any that keep to these rules, and one draw needn't show every extreme that they name: `block_hamiltonian`: each block is a symmetric matrix.
All inputs are finite; a program needn't handle non-finite values.
Results may differ from the reference program's by a relative error of at most 0.0085.
Values may be sent and summed in bfloat16 or wider, within the bound.
A program may use at most 128 MiB of HBM per device.

```python
import math
import jax
import jax.numpy as jnp
from jax import lax

STATES = 6144
CHANNELS = 24
DELAYS = 64
TERMS = 4
BLOCKS = 8
RADIAL = 2048


def draw_block_hamiltonian(key, part):
    keys = jax.random.split(key, BLOCKS)

    def make_block(one_key):
        random_part = jax.random.normal(one_key, (STATES, STATES), jnp.float32)
        symmetric = (random_part + random_part.T) / math.sqrt(2.0 * STATES)
        energies = jax.random.uniform(jax.random.fold_in(one_key, 7), (STATES,), jnp.float32, -1.0, 1.0)
        return (symmetric + jnp.diag(energies)).astype(jnp.bfloat16)
    return lax.map(make_block, keys)


def set_ends(values, own_key, smallest, high):
    shape = values.shape
    place = [jax.random.randint(jax.random.fold_in(own_key, axis), (), 0, shape[axis]) for axis in range(len(shape))]
    values = values.at[tuple(place)].set(smallest)
    longest = shape.index(max(shape))
    place[longest] = (place[longest] + 1) % shape[longest]
    return values.at[tuple(place)].set(high)


def steps_of(rng, shape, shards, least, largest):
    factor_of = 1.0
    for position, blocks in shards:
        draws = jax.random.uniform(jax.random.fold_in(jax.random.fold_in(rng, 6), position), (blocks,), jnp.float32, least / len(shards), largest / len(shards))
        factor_of = factor_of * jnp.repeat(jnp.exp(draws), shape[position] // blocks).reshape((-1,) + (1,) * (len(shape) - 1 - position))
    return factor_of


def bell_draw(own_key, shape, deviation, limit, cuts=(), kind=jnp.bfloat16):
    values = jax.random.normal(own_key, shape, jnp.float32) * deviation
    if len(cuts) > 0:
        values = steps_of(own_key, shape, cuts, -0.22, 0.18) * values
    return jnp.clip(values, min=-limit, max=limit).astype(kind)


def setup_inputs(seed: int = 0) -> dict:
    arg_keys = jax.random.split(jax.random.key(seed), 11)
    return {
        "inner_state": bell_draw(arg_keys[0], (BLOCKS, STATES, 2 * DELAYS), 1.0, 6.0, ((0, 8), (1, 16)), jnp.float32),
        "outer_state": bell_draw(arg_keys[1], (BLOCKS, CHANNELS, 2 * DELAYS, RADIAL), 1.0, 6.0, ((0, 8), (3, 16)), jnp.float32),
        "block_hamiltonian": draw_block_hamiltonian(jax.random.fold_in(arg_keys[10], 71), 0),
        "dipole": bell_draw(arg_keys[3], (BLOCKS, STATES, STATES), STATES ** -0.5, 0.078125, ((0, 8), (1, 16))),
        "field_strength": bell_draw(arg_keys[4], (DELAYS,), 0.3, 1.2, (), jnp.float32),
        "dipole_links": set_ends((jax.random.randint(arg_keys[5], (BLOCKS - 1, DELAYS), 0, 2) < 1).astype(jnp.int32), jax.random.fold_in(arg_keys[5], 1), 0, 1),
        "ghost_amplitude": bell_draw(arg_keys[6], (BLOCKS, 2, STATES), 0.0625, 0.4, ((0, 8),), jnp.float32),
        "surface_amplitude": bell_draw(arg_keys[7], (BLOCKS, STATES), 0.5, 3.0, ((0, 8),), jnp.float32),
        "state_channel": set_ends(jax.random.randint(arg_keys[8], (BLOCKS, STATES), 0, CHANNELS), jax.random.fold_in(arg_keys[8], 1), 0, CHANNELS - 1).astype(jnp.int32),
        "threshold": jnp.clip(1.0 * jax.random.uniform(arg_keys[9], (BLOCKS, CHANNELS), jnp.float32) ** steps_of(arg_keys[9], (BLOCKS, CHANNELS), ((0, 8),), -0.2, 0.2), 0.0, 1.0),
    }


time_step = 2.0
spacing = 1.5
radius_start = 20.0
charge = 1.0


def plain_products(matrices, vectors):
    def single(operands):
        return jnp.dot(operands[0], operands[1], preferred_element_type=jnp.float32)
    return lax.map(single, (matrices, vectors))


def transposed_products(matrices, vectors):
    def single(operands):
        return jnp.dot(operands[0].T, operands[1], preferred_element_type=jnp.float32)
    return lax.map(single, (matrices, vectors))


def rotate(values, factor, axis):
    real_part, imag_part = jnp.split(values, 2, axis=axis)
    return jnp.concatenate([factor * imag_part, -factor * real_part], axis=axis)


def reference(inner_state, outer_state, block_hamiltonian, dipole, field_strength, dipole_links, ghost_amplitude, surface_amplitude, state_channel, threshold):
    channel_hot = (state_channel[:, :, None] == jnp.arange(CHANNELS, dtype=jnp.int32)[None, None, :]).astype(jnp.float32)
    radius = radius_start + spacing * jnp.arange(RADIAL).astype(jnp.float32)
    potential = threshold[:, :, None] - charge / radius[None, None, :]
    column_field = jnp.concatenate([field_strength, field_strength])
    links_float = dipole_links.astype(jnp.float32)
    coupled = jnp.concatenate([links_float, jnp.zeros((1, links_float.shape[1]), jnp.float32)], axis=0)
    coupled = jnp.concatenate([coupled, coupled], axis=1)
    weighted = ghost_amplitude[:, :, :, None] * channel_hot[:, None, :, :]
    inner_vec = inner_state
    outer_vec = outer_state
    inner_total = inner_state
    outer_total = outer_state
    for order in range(1, TERMS + 1):
        rounded = inner_vec.astype(jnp.bfloat16)
        ghost = jnp.einsum('ljpc,lpq->ljcq', weighted, rounded.astype(jnp.float32), precision=lax.Precision.HIGHEST)
        slope = (outer_vec[:, :, :, 1] - ghost[:, 0]) / (2.0 * spacing)
        padded = jnp.concatenate([ghost[:, 1][..., None], ghost[:, 0][..., None], outer_vec,
                                  jnp.zeros(outer_vec.shape[:3] + (2,), jnp.float32)], axis=-1)
        laplace = (-padded[..., :-4] + 16.0 * padded[..., 1:-3] - 30.0 * padded[..., 2:-2]
                   + 16.0 * padded[..., 3:-1] - padded[..., 4:]) / (12.0 * spacing * spacing)
        outer_image = -0.5 * laplace + potential[:, :, None, :] * outer_vec
        hamiltonian_part = plain_products(block_hamiltonian, rounded)
        upper_vectors = jnp.concatenate([rounded[1:], jnp.zeros_like(rounded[:1])], axis=0)
        upper_part = plain_products(dipole, upper_vectors)
        lifted = transposed_products(dipole, rounded) * coupled[:, None, :]
        lower_part = jnp.concatenate([jnp.zeros_like(lifted[:1]), lifted[:-1]], axis=0)
        source = jnp.einsum('lpc,lcq->lpq', channel_hot, slope, precision=lax.Precision.HIGHEST)
        inner_image = (hamiltonian_part
                       + column_field[None, None, :] * (coupled[:, None, :] * upper_part + lower_part)
                       + 0.5 * surface_amplitude[:, :, None] * source)
        factor = time_step / order
        inner_vec = rotate(inner_image, factor, 2)
        outer_vec = rotate(outer_image, factor, 2)
        inner_total = inner_total + inner_vec
        outer_total = outer_total + outer_vec
    return inner_total, outer_total
```

```python
import jax
import jax.numpy as jnp
from jax import lax
from jax.experimental import pallas as pl
from jax.experimental.pallas import tpu as pltpu
from jax.sharding import PartitionSpec as P

TERMS = 4
time_step = 2.0
spacing = 1.5
radius_start = 20.0
charge = 1.0

MESH = pl.DeviceIdType.MESH
BF = jnp.bfloat16
F32 = jnp.float32

ROWS = 384
HALF = 192
STATES = 6144
KHALF = 3072
CH = 24
Q = 128
SLAB = 128
S0 = 15.0 / (12.0 * spacing * spacing)
S1 = -8.0 / (12.0 * spacing * spacing)
S2 = 0.5 / (12.0 * spacing * spacing)


def kernel(
    inner_hbm, outer_hbm, ham_hbm, dip_hbm, par_ref, ghost_ref, surf_ref, chan_ref, edge_ref,
    total_ref, outer_ref,
    uf, uo, uu, ut, pt, rl, hp, hr, up, ur, hg, dc, sh, slp,
    tl, tr, dl, dr, cs, ct, ab, invr, ghs,
    ss, rs, es_s, es_r, as_s, as_r, ms_s, ms_r, ls,
):
    s = lax.axis_index("sym")
    r = lax.axis_index("row")
    xh = r // 8
    z = (r // 2) % 4
    c = r % 2
    me = xh * 4 + z
    deltas = (1, 3, 2)

    def zz(d, sign=1):
        return (z + sign * deltas[d] + 4) % 4

    def dev(b, x, zc):
        return (b, x * 8 + zc * 2 + c)

    below = (s + 7) % 8
    above = (s + 1) % 8
    partner = (s, xh * 8 + z * 2 + (1 - c))
    zdev = [dev(s, xh, zz(d)) for d in range(3)]
    xdev = dev(s, 1 - xh, z)

    cin = pltpu.make_async_copy(inner_hbm, uf, ls.at[0])
    cin.start()

    def own_cols(k, core):
        return pl.ds(pl.multiple_of((2 * k + core) * ROWS, ROWS), ROWS)

    crow = pl.ds(pl.multiple_of(c * ROWS, ROWS), ROWS)

    def local_mat(src, dst, k, sem):
        return pltpu.make_async_copy(
            src.at[:, own_cols(k, c)], dst.at[crow, pl.ds(k * ROWS, ROWS)], sem
        )

    def remote_mat(src, dst, k, i):
        return pltpu.make_async_remote_copy(
            src_ref=src.at[:, own_cols(k, 1 - c)], dst_ref=dst.at[crow, pl.ds(k * ROWS, ROWS)],
            send_sem=ms_s.at[i, k], recv_sem=ms_r.at[i, k], device_id=partner, device_id_type=MESH,
        )

    for k in range(8):
        local_mat(dip_hbm, dc, k, ls.at[8 + k]).start()

    barrier = pltpu.get_barrier_semaphore()
    for j in range(1, 16):
        pl.semaphore_signal(barrier, inc=1, device_id=(s, (r + j) % 16), device_id_type=MESH)
    for t in range(8):
        pl.semaphore_signal(barrier, inc=1, device_id=dev(above, t // 4, t % 4), device_id_type=MESH)
        pl.semaphore_signal(barrier, inc=1, device_id=dev(below, t // 4, t % 4), device_id_type=MESH)
    pl.semaphore_wait(barrier, 31)

    for k in range(8):
        remote_mat(dip_hbm, dc, k, 0).start()

    def rc(o, src, dst, si, ri, device):
        return pltpu.make_async_remote_copy(
            src_ref=src, dst_ref=dst, send_sem=ss.at[o, si], recv_sem=rs.at[o, ri],
            device_id=device, device_id_type=MESH,
        )

    lo = pl.ds(0, HALF)
    hi = pl.ds(HALF, HALF)
    ccol = pl.ds(pl.multiple_of(c * ROWS, ROWS), ROWS)

    def m_core(o):
        return rc(o, ut.at[o, :, ccol], ut.at[o, :, ccol], 0, 0, partner)

    def m_own(o, d):
        ref = uo.at[o, xh, z]
        return rc(o, ref, ref, 1 + d, 1 + d, zdev[d] if d < 3 else xdev)

    def m_up(o, x):
        return rc(o, uo.at[o, xh, z], uu.at[o, xh, z], 5 + x, 5 + xh, dev(below, x, z))

    def m_f1(o, d):
        ref = uo.at[o, 1 - xh, z, lo]
        return rc(o, ref, ref, 7 + d, 7 + d, zdev[d])

    def m_f2(o, d):
        ref = uo.at[o, xh, zz(d, -1), hi]
        return rc(o, ref, ref, 10 + d, 10 + d, xdev)

    def m_f2u(o, d, x):
        return rc(o, uo.at[o, xh, zz(d, -1), hi], uu.at[o, xh, zz(d, -1), hi],
                  13 + x * 3 + d, 13 + xh * 3 + d, dev(below, x, z))

    def m_f3(o, d):
        ref = uu.at[o, :, z, lo]
        return rc(o, ref, ref, 19 + d, 19 + d, zdev[d])

    def m_low(o, t):
        return rc(o, pt.at[o, t], rl.at[o, me], 22 + t, 22 + me, dev(above, t // 4, t % 4))

    def m_hp(o):
        return rc(o, hp.at[o, 1 - c], hr.at[o], 30, 30, partner)

    def m_upp(o):
        return rc(o, up.at[o, 1 - c], ur.at[o], 31, 31, partner)

    def wr(o, dst, ri):
        rc(o, dst, dst, ri, ri, partner).wait_recv()

    def all_msgs(o):
        out = [m_core(o)]
        out += [m_own(o, d) for d in range(4)]
        out += [m_up(o, x) for x in range(2)]
        out += [m_f1(o, d) for d in range(3)] + [m_f2(o, d) for d in range(3)]
        out += [m_f2u(o, d, x) for x in range(2) for d in range(3)]
        out += [m_f3(o, d) for d in range(3)]
        out += [m_low(o, t) for t in range(8)]
        return out + [m_hp(o), m_upp(o)]

    right = (s, (r + 1) % 16)
    left = (s, (r + 15) % 16)

    def m_edge(i):
        src = edge_ref.at[pl.ds(8, 8)] if i == 0 else edge_ref.at[pl.ds(0, 8)]
        dst = tl.at[pl.ds(0, 8)] if i == 0 else tr.at[pl.ds(8, 8)]
        return pltpu.make_async_remote_copy(
            src_ref=src, dst_ref=dst, send_sem=es_s.at[i], recv_sem=es_r.at[i],
            device_id=right if i == 0 else left, device_id_type=MESH,
        )

    def m_first(j):
        return pltpu.make_async_remote_copy(
            src_ref=ab, dst_ref=ab, send_sem=as_s.at[j], recv_sem=as_r,
            device_id=(s, j), device_id_type=MESH,
        )

    lane = lax.broadcasted_iota(jnp.int32, (1, Q), 1)
    sign = jnp.where(lane < Q // 2, F32(1.0), F32(-1.0))

    def spin(x):
        return pltpu.roll(x, Q // 2, 1) * sign

    cin.wait()

    pos = lax.broadcasted_iota(jnp.int32, (32, Q), 0)
    pos = jnp.where(pos < 16, pos - 8, pos + 104) + r * SLAB
    invr[...] = charge / (radius_start + spacing * pos.astype(F32))
    thr = par_ref[0:CH, :]

    def image(two_low, low, mid, high, two_high, inv):
        return S2 * (two_low + two_high) + S1 * (low + high) + (S0 + thr - inv) * mid

    def inv_first(p):
        return charge / (radius_start + spacing * p)

    def factor_of(o):
        return jnp.where(o == 0, F32(2.0), jnp.where(o == 1, F32(1.0), jnp.where(o == 2, F32(2.0 / 3.0), F32(0.5))))

    total_ref[...] = uf[...]

    def send_first(o):
        u = uf[...]
        uo[o, xh, z] = u.astype(BF)
        for d in range(4):
            m_own(o, d).start()
        for x in range(2):
            m_up(o, x).start()
        ut[o, :, ccol] = jnp.transpose(u).astype(BF)
        m_core(o).start()

    send_first(0)
    m_edge(0).start()
    m_edge(1).start()

    @pl.when(r == 0)
    def _():
        zero = jnp.zeros((CH, Q), F32)
        strip = [edge_ref[p] for p in range(8)]
        ab[0] = strip[1]
        for k in range(1, TERMS):
            keep = 8 - 2 * k
            ext = [zero, zero] + strip
            strip = [
                (time_step / k) * spin(image(ext[p], ext[p + 1], ext[p + 2], ext[p + 3], ext[p + 4], inv_first(p)))
                for p in range(keep)
            ]
            ab[k] = strip[1]
        for j in range(1, 16):
            m_first(j).start()

    for k in range(8):
        local_mat(ham_hbm, hg, k, ls.at[16 + k]).start()
        remote_mat(ham_hbm, hg, k, 1).start()
    cout = pltpu.make_async_copy(outer_hbm, outer_ref, ls.at[1])
    cout.start()

    for k in range(8):
        cols = own_cols(k, c)
        hot = chan_ref[0:1, cols] == lax.broadcasted_iota(jnp.int32, (CH, ROWS), 0)
        for j in range(2):
            g = jnp.where(hot, ghost_ref[j:j + 1, cols], F32(0.0))
            top = g.astype(BF)
            hg[768 + j * CH:768 + (j + 1) * CH, k * ROWS:(k + 1) * ROWS] = top
            hg[816 + j * CH:816 + (j + 1) * CH, k * ROWS:(k + 1) * ROWS] = (g - top.astype(F32)).astype(BF)
    mine = pl.ds(pl.multiple_of(r * ROWS, ROWS), ROWS)
    hot = chan_ref[0:1, mine] == lax.broadcasted_iota(jnp.int32, (Q, ROWS), 0)
    sh[...] = jnp.transpose(jnp.where(hot, 0.5 * surf_ref[0:1, mine], F32(0.0)))
    slp[...] = jnp.zeros_like(slp)
    for ref in (dl, dr, cs, ct):
        ref[...] = jnp.zeros_like(ref)
    tl[8:16] = edge_ref[0:8]
    tr[0:8] = edge_ref[8:16]

    col_upper = par_ref[CH:CH + 1, :]
    col_lower = par_ref[CH + 1:CH + 2, :]
    pos_lane = (lax.broadcasted_iota(jnp.int32, (1, SLAB), 1) + r * SLAB).astype(F32)
    lane_inv = charge / (radius_start + spacing * pos_lane)

    def outer_channel(ch):
        w = outer_ref[ch]
        acc = w
        mid = (S0 + par_ref[pl.ds(ch, 1), :]) - lane_inv
        for k in range(1, TERMS + 1):
            p1 = jnp.where(lane >= 1, pltpu.roll(w, 1, 1), 0.0)
            p2 = jnp.where(lane >= 2, pltpu.roll(w, 2, 1), 0.0)
            n1 = jnp.where(lane < SLAB - 1, pltpu.roll(w, SLAB - 1, 1), 0.0)
            n2 = jnp.where(lane < SLAB - 2, pltpu.roll(w, SLAB - 2, 1), 0.0)
            img = S2 * (p2 + n2) + S1 * (p1 + n1) + mid * w
            f = time_step / k
            w = jnp.concatenate([f * img[Q // 2:], -f * img[:Q // 2]], axis=0)
            acc = acc + w
        outer_ref[ch] = acc

    def order(o, carry):
        factor = factor_of(o)

        @pl.when(o > 0)
        def _():
            send_first(o)

        @pl.when(o == 0)
        def _():
            for k in range(8):
                local_mat(dip_hbm, dc, k, ls.at[8 + k]).wait()
                remote_mat(dip_hbm, dc, k, 0).wait_recv()

        wr(o, ut.at[o, :, ccol], 0)
        both = ut[o]
        for pair in range(4):
            prod = jnp.dot(both, dc[:, pair * 768:(pair + 1) * 768], preferred_element_type=F32)
            for j in range(2):
                pt[o, pair * 2 + j] = prod[:, j * ROWS:(j + 1) * ROWS].astype(BF)
                m_low(o, pair * 2 + j).start()

        for d in range(2):
            wr(o, uo.at[o, xh, zz(d, -1)], 1 + d)
            m_f2(o, d).start()
            for x in range(2):
                m_f2u(o, d, x).start()
        wr(o, uo.at[o, 1 - xh, z], 4)
        for d in range(3):
            m_f1(o, d).start()
        for x in range(2):
            wr(o, uu.at[o, x, z], 5 + x)
        for d in range(3):
            m_f3(o, d).start()
        wr(o, uo.at[o, xh, zz(2, -1)], 3)
        m_f2(o, 2).start()
        for x in range(2):
            m_f2u(o, 2, x).start()

        @pl.when(o == 0)
        def _():
            for k in range(8):
                local_mat(ham_hbm, hg, k, ls.at[16 + k]).wait()
                remote_mat(ham_hbm, hg, k, 1).wait_recv()
            cout.wait()
            m_edge(0).wait_recv()
            m_edge(1).wait_recv()

        def chans(j, carry):
            outer_channel(o * 6 + j)
            return carry

        lax.fori_loop(0, 6, chans, 0)

        for d in range(3):
            wr(o, uo.at[o, 1 - xh, zz(d, -1), lo], 7 + d)
            wr(o, uo.at[o, 1 - xh, zz(d, -1), hi], 10 + d)
        prod = jnp.dot(hg[...], uo[o].reshape(KHALF, Q), preferred_element_type=F32)
        gpart = prod[768:816] + prod[816:864]
        for j in range(2):
            hp[o, j, 0:ROWS] = prod[j * ROWS:(j + 1) * ROWS]
            hp[o, j, ROWS:ROWS + 48] = gpart
        m_hp(o).start()

        for d in range(3):
            for x in range(2):
                wr(o, uu.at[o, x, zz(d, -1), hi], 13 + x * 3 + d)
            wr(o, uu.at[o, :, zz(d, -1), lo], 19 + d)
        prod = jnp.dot(dc[...], uu[o].reshape(KHALF, Q), preferred_element_type=F32)
        for j in range(2):
            up[o, j] = prod[j * ROWS:(j + 1) * ROWS]
        m_upp(o).start()

        wr(o, hr.at[o], 30)
        ghs[...] = hr[o, ROWS:ROWS + 48] + hp[o, c, ROWS:ROWS + 48]
        ghost0 = ghs[0:CH]
        ghost1 = ghs[CH:2 * CH]

        @pl.when((o == 0) & (r != 0))
        def _():
            m_first(1).wait_recv()

        slp[0:CH] = (ab[o] + cs[3] - ghost0) * (1.0 / (2.0 * spacing))
        source = jnp.dot(sh[...], slp[...], precision=lax.Precision.HIGHEST, preferred_element_type=F32)
        first = r == 0
        last = r == 15
        dl[0] = jnp.where(first, ghost1, tl[6])
        dl[1] = jnp.where(first, ghost0, tl[7])
        dr[10] = jnp.where(last, 0.0, tr[8])
        dr[11] = jnp.where(last, 0.0, tr[9])
        cs[0] = ghost1
        cs[1] = ghost0

        def advance(ref, first_index, count, inv):
            out = [
                factor * spin(image(ref[i - 2], ref[i - 1], ref[i], ref[i + 1], ref[i + 2], inv(i)))
                for i in range(first_index, first_index + count)
            ]
            for i in range(count):
                ref[first_index + i] = out[i]

        advance(tl, 2, 12, lambda i: invr[i:i + 1, :])
        advance(tr, 2, 12, lambda i: invr[16 + i:17 + i, :])
        advance(dl, 2, 8, lambda i: invr[6 + i:7 + i, :])
        advance(dr, 2, 8, lambda i: invr[14 + i:15 + i, :])
        advance(cs, 2, 8, lambda i: inv_first(i - 2))
        ct[0:8] = ct[0:8] + dl[2:10]
        ct[8:16] = ct[8:16] + dr[2:10]

        for k in range(8):
            wr(o, rl.at[o, k], 22 + k)
        low = rl[o, 0].astype(F32)
        for k in range(1, 8):
            low = low + rl[o, k].astype(F32)
        low = jnp.transpose(low)
        wr(o, ur.at[o], 31)
        img = (
            hp[o, c, 0:ROWS] + hr[o, 0:ROWS] + source
            + col_upper * (up[o, c] + ur[o])
            + jnp.where(s == 0, 0.0, col_lower * low)
        )
        new = factor * spin(img)
        uf[...] = new
        total_ref[...] = total_ref[...] + new
        return carry

    lax.fori_loop(0, TERMS, order, 0)

    def fix(ch, carry):
        rows = ct[:, pl.ds(ch, 1), :].reshape(16, Q)
        block = jnp.concatenate([rows[0:8], jnp.zeros((SLAB - 16, Q), F32), rows[8:16]], axis=0)
        outer_ref[ch] = outer_ref[ch] + jnp.transpose(block)
        return carry

    lax.fori_loop(0, CH, fix, 0)

    def drain(o, carry):
        for m in all_msgs(o):
            m.wait_send()
        return carry

    lax.fori_loop(0, TERMS, drain, 0)
    for k in range(8):
        remote_mat(dip_hbm, dc, k, 0).wait_send()
        remote_mat(ham_hbm, hg, k, 1).wait_send()
    m_edge(0).wait_send()
    m_edge(1).wait_send()

    @pl.when(r == 0)
    def _():
        for j in range(1, 16):
            m_first(j).wait_send()


def per_device(
    inner_state, outer_state, block_hamiltonian, dipole, field_strength, dipole_links,
    ghost_amplitude, surface_amplitude, state_channel, threshold,
):
    block_index = lax.axis_index("sym")
    links = jnp.pad(dipole_links.astype(F32), ((1, 1), (0, 0)))
    near = lax.dynamic_slice_in_dim(links, block_index, 2, 0)
    near = near[::-1] * field_strength[None, :]
    par = jnp.concatenate([
        jnp.broadcast_to(threshold[0][:, None], (CH, Q)),
        jnp.concatenate([near, near], axis=1),
        jnp.zeros((6, Q), F32),
    ], axis=0)
    outer = outer_state[0]
    edge = jnp.transpose(jnp.concatenate([outer[..., :8], outer[..., SLAB - 8:]], axis=-1), (2, 0, 1))
    any_ = pl.BlockSpec(memory_space=pl.ANY)
    vmem = pl.BlockSpec(memory_space=pltpu.VMEM)
    dma = pltpu.SemaphoreType.DMA
    inner_next, outer_next = pl.pallas_call(
        kernel,
        out_shape=(
            jax.ShapeDtypeStruct((ROWS, Q), F32),
            jax.ShapeDtypeStruct((CH, Q, SLAB), F32),
        ),
        in_specs=[any_] * 4 + [vmem] * 5,
        out_specs=(vmem, vmem),
        scratch_shapes=[
            pltpu.VMEM((ROWS, Q), F32),
            pltpu.VMEM((TERMS, 2, 4, ROWS, Q), BF),
            pltpu.VMEM((TERMS, 2, 4, ROWS, Q), BF),
            pltpu.VMEM((TERMS, Q, 2 * ROWS), BF),
            pltpu.VMEM((TERMS, 8, Q, ROWS), BF),
            pltpu.VMEM((TERMS, 8, Q, ROWS), BF),
            pltpu.VMEM((TERMS, 2, ROWS + 48, Q), F32),
            pltpu.VMEM((TERMS, ROWS + 48, Q), F32),
            pltpu.VMEM((TERMS, 2, ROWS, Q), F32),
            pltpu.VMEM((TERMS, ROWS, Q), F32),
            pltpu.VMEM((864, KHALF), BF),
            pltpu.VMEM((768, KHALF), BF),
            pltpu.VMEM((ROWS, Q), F32),
            pltpu.VMEM((Q, Q), F32),
            pltpu.VMEM((16, CH, Q), F32),
            pltpu.VMEM((16, CH, Q), F32),
            pltpu.VMEM((12, CH, Q), F32),
            pltpu.VMEM((12, CH, Q), F32),
            pltpu.VMEM((12, CH, Q), F32),
            pltpu.VMEM((16, CH, Q), F32),
            pltpu.VMEM((TERMS, CH, Q), F32),
            pltpu.VMEM((32, Q), F32),
            pltpu.VMEM((48, Q), F32),
            dma((TERMS, 32)), dma((TERMS, 32)),
            dma((2,)), dma((2,)),
            dma((16,)), dma,
            dma((2, 8)), dma((2, 8)),
            dma((24,)),
        ],
        compiler_params=pltpu.CompilerParams(
            collective_id=0, has_side_effects=True, vmem_limit_bytes=52 * 1024 * 1024
        ),
        name="propagate",
    )(
        inner_state[0], outer, block_hamiltonian[0], dipole[0], par,
        ghost_amplitude[0], surface_amplitude, state_channel, edge,
    )
    return inner_next[None], outer_next[None]


def solution(mesh):
    return jax.shard_map(
        per_device,
        mesh=mesh,
        in_specs=(
            P("sym", "row", None),
            P("sym", None, None, "row"),
            P("sym", "row", None),
            P("sym", "row", None),
            P(),
            P(),
            P("sym", None, None),
            P("sym", None),
            P("sym", None),
            P("sym", None),
        ),
        out_specs=(P("sym", "row", None), P("sym", None, None, "row")),
        check_vma=False,
    )
```

```python
import jax
import jax.numpy as jnp
from jax import lax
from jax.experimental import pallas as pl
from jax.experimental.pallas import tpu as pltpu
from jax.sharding import PartitionSpec as P

TERMS = 4
time_step = 2.0
spacing = 1.5
radius_start = 20.0
charge = 1.0

MESH = pl.DeviceIdType.MESH
BF = jnp.bfloat16
F32 = jnp.float32

ROWS = 384
FIRST = 96
STATES = 6144
KHALF = 3072
CH = 24
Q = 128
SLAB = 128
S0 = 15.0 / (12.0 * spacing * spacing)
S1 = -8.0 / (12.0 * spacing * spacing)
S2 = 0.5 / (12.0 * spacing * spacing)


def kernel(
    inner_hbm, outer_hbm, ham_hbm, dip_hbm, *rest,
):
    small_hbm, (total_hbm, outer_out, pack_hbm), scratch = rest[:6], rest[6:9], rest[9:]
    small, scratch = scratch[:6], scratch[6:]
    field_ref, link_ref, thr_ref, ghost_ref, surf_ref, chan_ref = small
    (
        total_ref, outer_ref, ct, pack,
        uf, uo, uu, ut, pt, rfar, rz, rsum, rl, acc, hp, hr, up, ur, hg, dc, sh, slp,
        edge_ref, thr_col, tl, tr, dl, dr, cs, ab, invr, ghs,
        ss, rs, es_s, es_r, as_s, as_r, ms_s, ms_r, ls,
    ) = scratch
    s = lax.axis_index("sym")
    r = lax.axis_index("row")
    xh = r // 8
    z = (r // 2) % 4
    c = r % 2
    deltas = (1, 3, 2)

    def zz(d, sign=1):
        return (z + sign * deltas[d] + 4) % 4

    def dev(b, x, zc):
        return (b, x * 8 + zc * 2 + c)

    below = (s + 7) % 8
    above = (s + 1) % 8
    partner = (s, xh * 8 + z * 2 + (1 - c))
    zdev = [dev(s, xh, zz(d)) for d in range(3)]
    xdev = dev(s, 1 - xh, z)

    cin = pltpu.make_async_copy(inner_hbm, uf, ls.at[0])
    cin.start()
    csmall = [pltpu.make_async_copy(small_hbm[i], small[i], ls.at[2 + i]) for i in range(6)]
    for copy in csmall:
        copy.start()

    def own_cols(k, core):
        return pl.ds(pl.multiple_of((2 * k + core) * ROWS, ROWS), ROWS)

    crow = pl.ds(pl.multiple_of(c * ROWS, ROWS), ROWS)

    def local_mat(src, dst, k, sem):
        return pltpu.make_async_copy(
            src.at[:, own_cols(k, c)], dst.at[crow, pl.ds(k * ROWS, ROWS)], sem
        )

    def remote_mat(src, dst, k, i):
        return pltpu.make_async_remote_copy(
            src_ref=src.at[:, own_cols(k, 1 - c)], dst_ref=dst.at[crow, pl.ds(k * ROWS, ROWS)],
            send_sem=ms_s.at[i, k], recv_sem=ms_r.at[i, k], device_id=partner, device_id_type=MESH,
        )

    for k in range(8):
        local_mat(dip_hbm, dc, k, ls.at[8 + k]).start()
    cout = pltpu.make_async_copy(outer_hbm, outer_ref, ls.at[1])
    cout.start()

    barrier = pltpu.get_barrier_semaphore()
    for j in range(1, 16):
        pl.semaphore_signal(barrier, inc=1, device_id=(s, (r + j) % 16), device_id_type=MESH)
    for x in range(2):
        pl.semaphore_signal(barrier, inc=1, device_id=dev(above, x, z), device_id_type=MESH)
        pl.semaphore_signal(barrier, inc=1, device_id=dev(below, x, z), device_id_type=MESH)
    pl.semaphore_wait(barrier, 19)

    for k in range(8):
        remote_mat(dip_hbm, dc, k, 0).start()

    def rc(o, src, dst, si, ri, device):
        return pltpu.make_async_remote_copy(
            src_ref=src, dst_ref=dst, send_sem=ss.at[o, si], recv_sem=rs.at[o, ri],
            device_id=device, device_id_type=MESH,
        )

    lo = pl.ds(0, FIRST)
    hi = pl.ds(FIRST, ROWS - FIRST)
    ccol = pl.ds(pl.multiple_of(c * ROWS, ROWS), ROWS)

    def m_core(o):
        return rc(o, ut.at[o, :, ccol], ut.at[o, :, ccol], 0, 0, partner)

    def m_own(o, d):
        ref = uo.at[o, xh, z]
        return rc(o, ref, ref, 1 + d, 1 + d, zdev[d] if d < 3 else xdev)

    def m_up(o, x):
        return rc(o, uo.at[o, xh, z], uu.at[o, xh, z], 5 + x, 5 + xh, dev(below, x, z))

    def m_f1(o, d):
        ref = uo.at[o, 1 - xh, z, lo]
        return rc(o, ref, ref, 7 + d, 7 + d, zdev[d])

    def m_f2(o, d):
        ref = uo.at[o, xh, zz(d, -1), hi]
        return rc(o, ref, ref, 10 + d, 10 + d, xdev)

    def m_f2u(o, d, x):
        return rc(o, uo.at[o, xh, zz(d, -1), hi], uu.at[o, xh, zz(d, -1), hi],
                  13 + x * 3 + d, 13 + xh * 3 + d, dev(below, x, z))

    def m_f3(o, d):
        ref = uu.at[o, :, z, lo]
        return rc(o, ref, ref, 19 + d, 19 + d, zdev[d])

    half = Q // 2
    part = (pl.ds(0, half), pl.ds(half, half))

    def m_far(o, d):
        return rc(o, pt.at[o, :, zz(2), part[d]], rfar.at[o, d], 22 + d, 22 + d, zdev[d])

    def m_near(o, d):
        return rc(o, pt.at[o, :, zz(d), part[1 - d]], rz.at[o, d, :, part[1 - d]], 27 + d, 27 + d, zdev[d])

    def m_both(o, d):
        return rc(o, pt.at[o, :, zz(d), part[d]], rz.at[o, d, :, part[d]], 32 + d, 32 + d, zdev[d])

    def m_lowx(o, x):
        return rc(o, rsum.at[o, x], rl.at[o, xh], 25 + x, 25 + xh, dev(above, x, z))

    def m_hp(o):
        return rc(o, hp.at[o, 1 - c], hr.at[o], 30, 30, partner)

    def m_upp(o):
        return rc(o, up.at[o, 1 - c], ur.at[o], 31, 31, partner)

    def wr(o, dst, ri):
        rc(o, dst, dst, ri, ri, partner).wait_recv()

    def all_msgs(o):
        out = [m_core(o)]
        out += [m_own(o, d) for d in range(4)]
        out += [m_up(o, x) for x in range(2)]
        out += [m_f1(o, d) for d in range(3)] + [m_f2(o, d) for d in range(3)]
        out += [m_f2u(o, d, x) for x in range(2) for d in range(3)]
        out += [m_f3(o, d) for d in range(3)]
        out += [m(o, d) for d in range(2) for m in (m_far, m_near, m_both, m_lowx)]
        return out + [m_hp(o), m_upp(o)]

    right = (s, (r + 1) % 16)
    left = (s, (r + 15) % 16)

    def m_edge(i):
        src = edge_ref.at[pl.ds(8, 8)] if i == 0 else edge_ref.at[pl.ds(0, 8)]
        dst = tl.at[pl.ds(0, 8)] if i == 0 else tr.at[pl.ds(8, 8)]
        return pltpu.make_async_remote_copy(
            src_ref=src, dst_ref=dst, send_sem=es_s.at[i], recv_sem=es_r.at[i],
            device_id=right if i == 0 else left, device_id_type=MESH,
        )

    def m_first(j):
        return pltpu.make_async_remote_copy(
            src_ref=ab, dst_ref=ab, send_sem=as_s.at[j], recv_sem=as_r,
            device_id=(s, j), device_id_type=MESH,
        )

    lane = lax.broadcasted_iota(jnp.int32, (1, Q), 1)
    sign = jnp.where(lane < Q // 2, F32(1.0), F32(-1.0))

    def spin(x):
        return pltpu.roll(x, Q // 2, 1) * sign

    cin.wait()

    for copy in csmall:
        copy.wait()
    pos = lax.broadcasted_iota(jnp.int32, (32, Q), 0)
    pos = jnp.where(pos < 16, pos - 8, pos + 104) + r * SLAB
    invr[...] = charge / (radius_start + spacing * pos.astype(F32))
    square = (CH, CH)
    eye = lax.broadcasted_iota(jnp.int32, square, 0) == lax.broadcasted_iota(jnp.int32, square, 1)
    column = jnp.sum(jnp.where(eye, jnp.broadcast_to(thr_ref[0:1, :], square), 0.0), axis=1, keepdims=True)
    thr_col[...] = jnp.broadcast_to(column, (CH, Q))
    thr = thr_col[...]

    def image(two_low, low, mid, high, two_high, inv):
        return S2 * (two_low + two_high) + S1 * (low + high) + (S0 + thr - inv) * mid

    def inv_first(p):
        return charge / (radius_start + spacing * p)

    def factor_of(o):
        return jnp.where(o == 0, F32(2.0), jnp.where(o == 1, F32(1.0), jnp.where(o == 2, F32(2.0 / 3.0), F32(0.5))))

    total_ref[...] = uf[...]

    def send_first(o):
        u = uf[...]
        uo[o, xh, z] = u.astype(BF)
        for d in range(4):
            m_own(o, d).start()
        for x in range(2):
            m_up(o, x).start()
        ut[o, :, ccol] = jnp.transpose(u).astype(BF)
        m_core(o).start()

    send_first(0)
    for k in range(8):
        local_mat(ham_hbm, hg, k, ls.at[16 + k]).start()
        remote_mat(ham_hbm, hg, k, 1).start()
    cout.wait()

    def edges(g, carry):
        block = jnp.zeros((Q, SLAB), F32)
        for j in range(8):
            turned = pltpu.roll(outer_ref[g * 8 + j], (16 * j + 8) % SLAB, 1)
            block = jnp.where((lane >= 16 * j) & (lane < 16 * j + 16), turned, block)
        pack[pl.ds(pl.multiple_of(g * SLAB, SLAB), SLAB)] = jnp.transpose(block)
        return carry

    lax.fori_loop(0, CH // 8, edges, 0)

    def packed(p):
        return pl.ds((p + 8) % 16, CH, stride=16)

    for p in range(16):
        edge_ref[p] = pack[packed(p), :]
    m_edge(0).start()
    m_edge(1).start()

    @pl.when(r == 0)
    def _():
        zero = jnp.zeros((CH, Q), F32)
        strip = [edge_ref[p] for p in range(8)]
        ab[0] = strip[1]
        for k in range(1, TERMS):
            keep = 8 - 2 * k
            ext = [zero, zero] + strip
            strip = [
                (time_step / k) * spin(image(ext[p], ext[p + 1], ext[p + 2], ext[p + 3], ext[p + 4], inv_first(p)))
                for p in range(keep)
            ]
            ab[k] = strip[1]
        for j in range(1, 16):
            m_first(j).start()

    for k in range(8):
        cols = own_cols(k, c)
        hot = chan_ref[0:1, cols] == lax.broadcasted_iota(jnp.int32, (CH, ROWS), 0)
        for j in range(2):
            g = jnp.where(hot, ghost_ref[j:j + 1, cols], F32(0.0))
            top = g.astype(BF)
            hg[768 + j * CH:768 + (j + 1) * CH, k * ROWS:(k + 1) * ROWS] = top
            hg[816 + j * CH:816 + (j + 1) * CH, k * ROWS:(k + 1) * ROWS] = (g - top.astype(F32)).astype(BF)
    mine = pl.ds(pl.multiple_of(r * ROWS, ROWS), ROWS)
    hot = chan_ref[0:1, mine] == lax.broadcasted_iota(jnp.int32, (Q, ROWS), 0)
    sh[...] = jnp.transpose(jnp.where(hot, 0.5 * surf_ref[0:1, mine], F32(0.0)))
    slp[...] = jnp.zeros_like(slp)
    for ref in (dl, dr, cs, ct):
        ref[...] = jnp.zeros_like(ref)
    tl[8:16] = edge_ref[0:8]
    tr[0:8] = edge_ref[8:16]

    def doubled(x):
        return jnp.concatenate([x, x], axis=1)

    def coupled_field(b):
        row = link_ref[pl.ds(jnp.clip(b, 0, 6), 1), :].astype(F32) * field_ref[...]
        return doubled(jnp.where((b >= 0) & (b < 7), row, 0.0))

    col_upper = coupled_field(s)
    col_lower = coupled_field(s - 1)
    pos_lane = (lax.broadcasted_iota(jnp.int32, (1, SLAB), 1) + r * SLAB).astype(F32)
    lane_inv = charge / (radius_start + spacing * pos_lane)

    def outer_channel(ch):
        w = outer_ref[ch]
        acc = w
        mid = (S0 + thr_col[pl.ds(ch, 1), :]) - lane_inv
        for k in range(1, TERMS + 1):
            p1 = jnp.where(lane >= 1, pltpu.roll(w, 1, 1), 0.0)
            p2 = jnp.where(lane >= 2, pltpu.roll(w, 2, 1), 0.0)
            n1 = jnp.where(lane < SLAB - 1, pltpu.roll(w, SLAB - 1, 1), 0.0)
            n2 = jnp.where(lane < SLAB - 2, pltpu.roll(w, SLAB - 2, 1), 0.0)
            img = S2 * (p2 + n2) + S1 * (p1 + n1) + mid * w
            f = time_step / k
            w = jnp.concatenate([f * img[Q // 2:], -f * img[:Q // 2]], axis=0)
            acc = acc + w
        outer_ref[ch] = acc

    def order(o, carry):
        factor = factor_of(o)

        @pl.when(o > 0)
        def _():
            send_first(o)

        @pl.when(o == 0)
        def _():
            for k in range(8):
                local_mat(dip_hbm, dc, k, ls.at[8 + k]).wait()
                remote_mat(dip_hbm, dc, k, 0).wait_recv()

        wr(o, ut.at[o, :, ccol], 0)
        both = ut[o]
        for pair in range(4):
            prod = jnp.dot(both, dc[:, pair * 768:(pair + 1) * 768], preferred_element_type=F32)
            for j in range(2):
                k = pair * 2 + j
                pt[o, k // 4, k % 4] = prod[:, j * ROWS:(j + 1) * ROWS].astype(BF)
        for d in range(2):
            m_far(o, d).start()
        for d in range(2):
            m_near(o, d).start()

        for d in range(2):
            wr(o, uo.at[o, xh, zz(d, -1)], 1 + d)
            m_f2(o, d).start()
            for x in range(2):
                m_f2u(o, d, x).start()
        wr(o, uo.at[o, 1 - xh, z], 4)
        for d in range(3):
            m_f1(o, d).start()
        for x in range(2):
            wr(o, uu.at[o, x, z], 5 + x)
        for d in range(3):
            m_f3(o, d).start()
        wr(o, uo.at[o, xh, zz(2, -1)], 3)
        m_f2(o, 2).start()
        for x in range(2):
            m_f2u(o, 2, x).start()
        for d in range(2):
            wr(o, rfar.at[o, d], 22 + d)
            rows = slice(d * half, (d + 1) * half)
            for x in range(2):
                pt[o, x, zz(d), rows] = (pt[o, x, zz(d), rows].astype(F32) + rfar[o, d, x].astype(F32)).astype(BF)
            m_both(o, d).start()

        @pl.when(o == 0)
        def _():
            for k in range(8):
                local_mat(ham_hbm, hg, k, ls.at[16 + k]).wait()
                remote_mat(ham_hbm, hg, k, 1).wait_recv()
            m_edge(0).wait_recv()
            m_edge(1).wait_recv()

        def chans(j, carry):
            outer_channel(o * 6 + j)
            return carry

        lax.fori_loop(0, 6, chans, 0)

        @pl.when(o == TERMS - 1)
        def _():
            pltpu.make_async_copy(outer_ref, outer_out, ls.at[1]).start()

        near_cols = pl.ds(pl.multiple_of(xh * (KHALF // 2), KHALF // 2), KHALF // 2)
        far_cols = pl.ds(pl.multiple_of((1 - xh) * (KHALF // 2), KHALF // 2), KHALF // 2)
        acc[...] = jnp.dot(hg[:, near_cols], uo[o, xh].reshape(KHALF // 2, Q), preferred_element_type=F32)

        for d in range(2):
            wr(o, rz.at[o, d, :, part[1 - d]], 27 + d)
            wr(o, rz.at[o, d, :, part[d]], 32 + d)
        for x in range(2):
            low = pt[o, x, z].astype(F32) + rz[o, 0, x].astype(F32) + rz[o, 1, x].astype(F32)
            rsum[o, x] = low.astype(BF)
            m_lowx(o, x).start()

        for d in range(3):
            wr(o, uo.at[o, 1 - xh, zz(d, -1), lo], 7 + d)
            wr(o, uo.at[o, 1 - xh, zz(d, -1), hi], 10 + d)
        prod = acc[...] + jnp.dot(hg[:, far_cols], uo[o, 1 - xh].reshape(KHALF // 2, Q), preferred_element_type=F32)
        gpart = prod[768:816] + prod[816:864]
        for j in range(2):
            hp[o, j, 0:ROWS] = prod[j * ROWS:(j + 1) * ROWS]
            hp[o, j, ROWS:ROWS + 48] = gpart
        m_hp(o).start()

        for d in range(3):
            for x in range(2):
                wr(o, uu.at[o, x, zz(d, -1), hi], 13 + x * 3 + d)
            wr(o, uu.at[o, :, zz(d, -1), lo], 19 + d)
        prod = jnp.dot(dc[...], uu[o].reshape(KHALF, Q), preferred_element_type=F32)
        for j in range(2):
            up[o, j] = prod[j * ROWS:(j + 1) * ROWS]
        m_upp(o).start()

        wr(o, hr.at[o], 30)
        ghs[...] = hr[o, ROWS:ROWS + 48] + hp[o, c, ROWS:ROWS + 48]
        ghost0 = ghs[0:CH]
        ghost1 = ghs[CH:2 * CH]

        @pl.when((o == 0) & (r != 0))
        def _():
            m_first(1).wait_recv()

        slp[0:CH] = (ab[o] + cs[3] - ghost0) * (1.0 / (2.0 * spacing))
        source = jnp.dot(sh[...], slp[...], precision=lax.Precision.HIGHEST, preferred_element_type=F32)
        first = r == 0
        last = r == 15
        dl[0] = jnp.where(first, ghost1, tl[6])
        dl[1] = jnp.where(first, ghost0, tl[7])
        dr[10] = jnp.where(last, 0.0, tr[8])
        dr[11] = jnp.where(last, 0.0, tr[9])
        cs[0] = ghost1
        cs[1] = ghost0

        def advance(ref, first_index, count, inv):
            out = [
                factor * spin(image(ref[i - 2], ref[i - 1], ref[i], ref[i + 1], ref[i + 2], inv(i)))
                for i in range(first_index, first_index + count)
            ]
            for i in range(count):
                ref[first_index + i] = out[i]

        advance(tl, 2, 12, lambda i: invr[i:i + 1, :])
        advance(tr, 2, 12, lambda i: invr[16 + i:17 + i, :])
        advance(dl, 2, 8, lambda i: invr[6 + i:7 + i, :])
        advance(dr, 2, 8, lambda i: invr[14 + i:15 + i, :])
        advance(cs, 2, 8, lambda i: inv_first(i - 2))
        ct[0:8] = ct[0:8] + dl[2:10]
        ct[8:16] = ct[8:16] + dr[2:10]

        @pl.when(o == TERMS - 1)
        def _():
            for p in range(16):
                pack[packed(p), :] = ct[p]
            pltpu.make_async_copy(pack, pack_hbm, ls.at[2]).start()

        for x in range(2):
            wr(o, rl.at[o, x], 25 + x)
        low = jnp.transpose(rl[o, 0].astype(F32) + rl[o, 1].astype(F32))
        wr(o, ur.at[o], 31)
        img = (
            hp[o, c, 0:ROWS] + hr[o, 0:ROWS] + source
            + col_upper * (up[o, c] + ur[o])
            + jnp.where(s == 0, 0.0, col_lower * low)
        )
        new = factor * spin(img)
        uf[...] = new
        total_ref[...] = total_ref[...] + new
        return carry

    lax.fori_loop(0, TERMS, order, 0)

    cend = pltpu.make_async_copy(total_ref, total_hbm, ls.at[0])
    cend.start()

    def drain(o, carry):
        for m in all_msgs(o):
            m.wait_send()
        return carry

    lax.fori_loop(0, TERMS, drain, 0)
    for k in range(8):
        remote_mat(dip_hbm, dc, k, 0).wait_send()
        remote_mat(ham_hbm, hg, k, 1).wait_send()
    m_edge(0).wait_send()
    m_edge(1).wait_send()
    pltpu.make_async_copy(outer_ref, outer_out, ls.at[1]).wait()
    pltpu.make_async_copy(pack, pack_hbm, ls.at[2]).wait()
    cend.wait()

    @pl.when(r == 0)
    def _():
        for j in range(1, 16):
            m_first(j).wait_send()


def finish(total_ref, outer_ref, pack_ref, inner_out, outer_out):
    inner_out[...] = total_ref[...]
    lane = lax.broadcasted_iota(jnp.int32, (1, SLAB), 1)
    block = jnp.transpose(pack_ref[...])
    for j in range(8):
        turned = pltpu.roll(block, (SLAB - 16 * j - 8) % SLAB, 1)
        outer_out[j] = outer_ref[j] + jnp.where((lane < 8) | (lane >= SLAB - 8), turned, 0.0)


def per_device(
    inner_state, outer_state, block_hamiltonian, dipole, field_strength, dipole_links,
    ghost_amplitude, surface_amplitude, state_channel, threshold,
):
    any_ = pl.BlockSpec(memory_space=pl.ANY)
    dma = pltpu.SemaphoreType.DMA
    total, outer, pack = pl.pallas_call(
        kernel,
        out_shape=(
            jax.ShapeDtypeStruct((ROWS, Q), F32),
            jax.ShapeDtypeStruct((CH, Q, SLAB), F32),
            jax.ShapeDtypeStruct((CH * 16, Q), F32),
        ),
        in_specs=[any_] * 10,
        out_specs=(any_,) * 3,
        scratch_shapes=[
            pltpu.VMEM((1, Q // 2), F32),
            pltpu.VMEM((7, Q // 2), jnp.int32),
            pltpu.VMEM((1, CH), F32),
            pltpu.VMEM((2, STATES), F32),
            pltpu.VMEM((1, STATES), F32),
            pltpu.VMEM((1, STATES), jnp.int32),
            pltpu.VMEM((ROWS, Q), F32),
            pltpu.VMEM((CH, Q, SLAB), F32),
            pltpu.VMEM((16, CH, Q), F32),
            pltpu.VMEM((CH * 16, Q), F32),
            pltpu.VMEM((ROWS, Q), F32),
            pltpu.VMEM((TERMS, 2, 4, ROWS, Q), BF),
            pltpu.VMEM((TERMS, 2, 4, ROWS, Q), BF),
            pltpu.VMEM((TERMS, Q, 2 * ROWS), BF),
            pltpu.VMEM((TERMS, 2, 4, Q, ROWS), BF),
            pltpu.VMEM((TERMS, 2, 2, Q // 2, ROWS), BF),
            pltpu.VMEM((TERMS, 2, 2, Q, ROWS), BF),
            pltpu.VMEM((TERMS, 2, Q, ROWS), BF),
            pltpu.VMEM((TERMS, 2, Q, ROWS), BF),
            pltpu.VMEM((864, Q), F32),
            pltpu.VMEM((TERMS, 2, ROWS + 48, Q), F32),
            pltpu.VMEM((TERMS, ROWS + 48, Q), F32),
            pltpu.VMEM((TERMS, 2, ROWS, Q), F32),
            pltpu.VMEM((TERMS, ROWS, Q), F32),
            pltpu.VMEM((864, KHALF), BF),
            pltpu.VMEM((768, KHALF), BF),
            pltpu.VMEM((ROWS, Q), F32),
            pltpu.VMEM((Q, Q), F32),
            pltpu.VMEM((16, CH, Q), F32),
            pltpu.VMEM((CH, Q), F32),
            pltpu.VMEM((16, CH, Q), F32),
            pltpu.VMEM((16, CH, Q), F32),
            pltpu.VMEM((12, CH, Q), F32),
            pltpu.VMEM((12, CH, Q), F32),
            pltpu.VMEM((12, CH, Q), F32),
            pltpu.VMEM((TERMS, CH, Q), F32),
            pltpu.VMEM((32, Q), F32),
            pltpu.VMEM((48, Q), F32),
            dma((TERMS, 34)), dma((TERMS, 34)),
            dma((2,)), dma((2,)),
            dma((16,)), dma,
            dma((2, 8)), dma((2, 8)),
            dma((24,)),
        ],
        compiler_params=pltpu.CompilerParams(
            collective_id=0, has_side_effects=True, vmem_limit_bytes=62 * 1024 * 1024
        ),
        name="propagate",
    )(
        inner_state[0], outer_state[0], block_hamiltonian[0], dipole[0], field_strength[None],
        dipole_links, threshold, ghost_amplitude[0], surface_amplitude, state_channel,
    )
    rows_spec = pl.BlockSpec((ROWS // 3, Q), lambda i: (i, 0))
    channels_spec = pl.BlockSpec((8, Q, SLAB), lambda i: (i, 0, 0))
    inner_next, outer_next = pl.pallas_call(
        finish,
        grid=(CH // 8,),
        out_shape=(
            jax.ShapeDtypeStruct((ROWS, Q), F32),
            jax.ShapeDtypeStruct((CH, Q, SLAB), F32),
        ),
        in_specs=[rows_spec, channels_spec, rows_spec],
        out_specs=(rows_spec, channels_spec),
        name="finish",
    )(total, outer, pack)
    return inner_next[None], outer_next[None]


def solution(mesh):
    return jax.shard_map(
        per_device,
        mesh=mesh,
        in_specs=(
            P("sym", "row", None),
            P("sym", None, None, "row"),
            P("sym", "row", None),
            P("sym", "row", None),
            P(),
            P(),
            P("sym", None, None),
            P("sym", None),
            P("sym", None),
            P("sym", None),
        ),
        out_specs=(P("sym", "row", None), P("sym", None, None, "row")),
        check_vma=False,
    )
```

```python
import jax
import jax.numpy as jnp
from jax import lax
from jax.experimental import pallas as pl
from jax.experimental.pallas import tpu as pltpu
from jax.sharding import PartitionSpec as P

TERMS = 4
time_step = 2.0
spacing = 1.5
radius_start = 20.0
charge = 1.0

MESH = pl.DeviceIdType.MESH
BF = jnp.bfloat16
F32 = jnp.float32

ROWS = 384
FIRST = 48
FIRST_UP = 192
STATES = 6144
KHALF = 3072
CH = 24
Q = 128
SLAB = 128
S0 = 15.0 / (12.0 * spacing * spacing)
S1 = -8.0 / (12.0 * spacing * spacing)
S2 = 0.5 / (12.0 * spacing * spacing)


def kernel(
    inner_hbm, outer_hbm, ham_hbm, dip_hbm, *rest,
):
    small_hbm, (total_hbm, outer_out), scratch = rest[:6], rest[6:8], rest[8:]
    small, scratch = scratch[:6], scratch[6:]
    field_ref, link_ref, thr_ref, ghost_ref, surf_ref, chan_ref = small
    (
        total_ref, outer_ref, ct, pack,
        uf, uo, uu, ut, pt, rfar, rz, rsum, rl, acc, accu, hp, hr, up, ur, hg, dc, sh, slp,
        edge_ref, thr_col, tl, tr, dl, dr, cs, ab, invr, ghs,
        ss, rs, es_s, es_r, as_s, as_r, ms_s, ms_r, ls,
    ) = scratch
    s = lax.axis_index("sym")
    r = lax.axis_index("row")
    xh = r // 8
    z = (r // 2) % 4
    c = r % 2
    deltas = (1, 3, 2)

    def zz(d, sign=1):
        return (z + sign * deltas[d] + 4) % 4

    def dev(b, x, zc):
        return (b, x * 8 + zc * 2 + c)

    below = (s + 7) % 8
    above = (s + 1) % 8
    partner = (s, xh * 8 + z * 2 + (1 - c))
    zdev = [dev(s, xh, zz(d)) for d in range(3)]
    xdev = dev(s, 1 - xh, z)

    cin = pltpu.make_async_copy(inner_hbm, uf, ls.at[0])
    cin.start()
    csmall = [pltpu.make_async_copy(small_hbm[i], small[i], ls.at[2 + i]) for i in range(6)]
    for copy in csmall:
        copy.start()

    def own_cols(k, core):
        return pl.ds(pl.multiple_of((2 * k + core) * ROWS, ROWS), ROWS)

    crow = pl.ds(pl.multiple_of(c * ROWS, ROWS), ROWS)

    def local_mat(src, dst, k, sem):
        return pltpu.make_async_copy(
            src.at[:, own_cols(k, c)], dst.at[crow, pl.ds(k * ROWS, ROWS)], sem
        )

    def remote_mat(src, dst, k, i):
        return pltpu.make_async_remote_copy(
            src_ref=src.at[:, own_cols(k, 1 - c)], dst_ref=dst.at[crow, pl.ds(k * ROWS, ROWS)],
            send_sem=ms_s.at[i, k], recv_sem=ms_r.at[i, k], device_id=partner, device_id_type=MESH,
        )

    for k in range(8):
        local_mat(dip_hbm, dc, k, ls.at[8 + k]).start()
    cout = pltpu.make_async_copy(outer_hbm, outer_ref, ls.at[1])
    cout.start()

    barrier = pltpu.get_barrier_semaphore()
    for j in range(1, 16):
        pl.semaphore_signal(barrier, inc=1, device_id=(s, (r + j) % 16), device_id_type=MESH)
    for x in range(2):
        pl.semaphore_signal(barrier, inc=1, device_id=dev(above, x, z), device_id_type=MESH)
        pl.semaphore_signal(barrier, inc=1, device_id=dev(below, x, z), device_id_type=MESH)
    pl.semaphore_wait(barrier, 19)

    for k in range(8):
        remote_mat(dip_hbm, dc, k, 0).start()

    def rc(o, src, dst, si, ri, device):
        return pltpu.make_async_remote_copy(
            src_ref=src, dst_ref=dst, send_sem=ss.at[o, si], recv_sem=rs.at[o, ri],
            device_id=device, device_id_type=MESH,
        )

    lo = pl.ds(0, FIRST)
    hi = pl.ds(FIRST, ROWS - FIRST)
    lo_up = pl.ds(0, FIRST_UP)
    hi_up = pl.ds(FIRST_UP, ROWS - FIRST_UP)
    ccol = pl.ds(pl.multiple_of(c * ROWS, ROWS), ROWS)

    def m_core(o):
        return rc(o, ut.at[o, :, ccol], ut.at[o, :, ccol], 0, 0, partner)

    def m_own(o, d):
        ref = uo.at[o, xh, z, hi if d < 3 else lo]
        return rc(o, ref, ref, 1 + d, 1 + d, zdev[d] if d < 3 else xdev)

    def m_own2(o, d):
        ref = uo.at[o, xh, z, lo if d < 3 else hi]
        return rc(o, ref, ref, 34 + d, 34 + d, zdev[d] if d < 3 else xdev)

    def m_up(o, x):
        return rc(o, uo.at[o, xh, z, lo_up], uu.at[o, xh, z, lo_up], 5 + x, 5 + xh, dev(below, x, z))

    def m_up2(o, x):
        return rc(o, uo.at[o, xh, z, hi_up], uu.at[o, xh, z, hi_up], 38 + x, 38 + xh, dev(below, x, z))

    def m_f1(o, d):
        ref = uo.at[o, 1 - xh, z, lo]
        return rc(o, ref, ref, 7 + d, 7 + d, zdev[d])

    def m_f2(o, d):
        ref = uo.at[o, xh, zz(d, -1), hi]
        return rc(o, ref, ref, 10 + d, 10 + d, xdev)

    def m_f2u(o, d, x):
        return rc(o, uo.at[o, xh, zz(d, -1), hi_up], uu.at[o, xh, zz(d, -1), hi_up],
                  13 + x * 3 + d, 13 + xh * 3 + d, dev(below, x, z))

    def m_f3(o, d):
        ref = uu.at[o, :, z, lo_up]
        return rc(o, ref, ref, 19 + d, 19 + d, zdev[d])

    half = Q // 2
    part = (pl.ds(0, half), pl.ds(half, half))

    def m_far(o, d):
        return rc(o, pt.at[o, :, zz(2), part[d]], rfar.at[o, d], 22 + d, 22 + d, zdev[d])

    def m_near(o, d):
        return rc(o, pt.at[o, :, zz(d), part[1 - d]], rz.at[o, d, :, part[1 - d]], 27 + d, 27 + d, zdev[d])

    def m_both(o, d):
        return rc(o, pt.at[o, :, zz(d), part[d]], rz.at[o, d, :, part[d]], 32 + d, 32 + d, zdev[d])

    def m_lowx(o, x):
        return rc(o, rsum.at[o, x], rl.at[o, xh], 25 + x, 25 + xh, dev(above, x, z))

    def m_hp(o):
        return rc(o, hp.at[o, 1 - c], hr.at[o], 30, 30, partner)

    def m_upp(o):
        return rc(o, up.at[o, 1 - c], ur.at[o], 31, 31, partner)

    def wr(o, dst, ri):
        rc(o, dst, dst, ri, ri, partner).wait_recv()

    def all_msgs(o):
        out = [m_core(o)]
        out += [m(o, d) for d in range(4) for m in (m_own, m_own2)]
        out += [m(o, x) for x in range(2) for m in (m_up, m_up2)]
        out += [m_f1(o, d) for d in range(3)] + [m_f2(o, d) for d in range(3)]
        out += [m_f2u(o, d, x) for x in range(2) for d in range(3)]
        out += [m_f3(o, d) for d in range(3)]
        out += [m(o, d) for d in range(2) for m in (m_far, m_near, m_both, m_lowx)]
        return out + [m_hp(o), m_upp(o)]

    right = (s, (r + 1) % 16)
    left = (s, (r + 15) % 16)

    def m_edge(i):
        src = edge_ref.at[pl.ds(8, 8)] if i == 0 else edge_ref.at[pl.ds(0, 8)]
        dst = tl.at[pl.ds(0, 8)] if i == 0 else tr.at[pl.ds(8, 8)]
        return pltpu.make_async_remote_copy(
            src_ref=src, dst_ref=dst, send_sem=es_s.at[i], recv_sem=es_r.at[i],
            device_id=right if i == 0 else left, device_id_type=MESH,
        )

    def m_first(j):
        return pltpu.make_async_remote_copy(
            src_ref=ab, dst_ref=ab, send_sem=as_s.at[j], recv_sem=as_r,
            device_id=(s, j), device_id_type=MESH,
        )

    lane = lax.broadcasted_iota(jnp.int32, (1, Q), 1)
    sign = jnp.where(lane < Q // 2, F32(1.0), F32(-1.0))

    def spin(x):
        return pltpu.roll(x, Q // 2, 1) * sign

    cin.wait()

    for copy in csmall:
        copy.wait()
    pos = lax.broadcasted_iota(jnp.int32, (32, Q), 0)
    pos = jnp.where(pos < 16, pos - 8, pos + 104) + r * SLAB
    invr[...] = charge / (radius_start + spacing * pos.astype(F32))
    square = (CH, CH)
    eye = lax.broadcasted_iota(jnp.int32, square, 0) == lax.broadcasted_iota(jnp.int32, square, 1)
    column = jnp.sum(jnp.where(eye, jnp.broadcast_to(thr_ref[0:1, :], square), 0.0), axis=1, keepdims=True)
    thr_col[...] = jnp.broadcast_to(column, (CH, Q))
    thr = thr_col[...]

    def image(two_low, low, mid, high, two_high, inv):
        return S2 * (two_low + two_high) + S1 * (low + high) + (S0 + thr - inv) * mid

    def inv_first(p):
        return charge / (radius_start + spacing * p)

    def factor_of(o):
        return jnp.where(o == 0, F32(2.0), jnp.where(o == 1, F32(1.0), jnp.where(o == 2, F32(2.0 / 3.0), F32(0.5))))

    total_ref[...] = uf[...]

    def send_first(o):
        u = uf[...]
        uo[o, xh, z] = u.astype(BF)
        for d in range(4):
            m_own(o, d).start()
        for x in range(2):
            m_up(o, x).start()
        ut[o, :, ccol] = jnp.transpose(u).astype(BF)
        m_core(o).start()

    send_first(0)
    for k in range(8):
        local_mat(ham_hbm, hg, k, ls.at[16 + k]).start()
        remote_mat(ham_hbm, hg, k, 1).start()
    cout.wait()

    def edges(g, carry):
        block = jnp.zeros((Q, SLAB), F32)
        for j in range(8):
            turned = pltpu.roll(outer_ref[g * 8 + j], (16 * j + 8) % SLAB, 1)
            block = jnp.where((lane >= 16 * j) & (lane < 16 * j + 16), turned, block)
        pack[pl.ds(pl.multiple_of(g * SLAB, SLAB), SLAB)] = jnp.transpose(block)
        return carry

    lax.fori_loop(0, CH // 8, edges, 0)

    def packed(p):
        return pl.ds((p + 8) % 16, CH, stride=16)

    for p in range(16):
        edge_ref[p] = pack[packed(p), :]
    m_edge(0).start()
    m_edge(1).start()

    @pl.when(r == 0)
    def _():
        zero = jnp.zeros((CH, Q), F32)
        strip = [edge_ref[p] for p in range(8)]
        ab[0] = strip[1]
        for k in range(1, TERMS):
            keep = 8 - 2 * k
            ext = [zero, zero] + strip
            strip = [
                (time_step / k) * spin(image(ext[p], ext[p + 1], ext[p + 2], ext[p + 3], ext[p + 4], inv_first(p)))
                for p in range(keep)
            ]
            ab[k] = strip[1]
        for j in range(1, 16):
            m_first(j).start()

    for ref in (dl, dr, cs, ct):
        ref[...] = jnp.zeros_like(ref)
    tl[8:16] = edge_ref[0:8]
    tr[0:8] = edge_ref[8:16]

    def doubled(x):
        return jnp.concatenate([x, x], axis=1)

    def coupled_field(b):
        row = link_ref[pl.ds(jnp.clip(b, 0, 6), 1), :].astype(F32) * field_ref[...]
        return doubled(jnp.where((b >= 0) & (b < 7), row, 0.0))

    col_upper = coupled_field(s)
    col_lower = coupled_field(s - 1)
    pos_lane = (lax.broadcasted_iota(jnp.int32, (1, SLAB), 1) + r * SLAB).astype(F32)
    lane_inv = charge / (radius_start + spacing * pos_lane)

    def outer_channel(ch):
        w = outer_ref[ch]
        acc = w
        mid = (S0 + thr_col[pl.ds(ch, 1), :]) - lane_inv
        for k in range(1, TERMS + 1):
            p1 = jnp.where(lane >= 1, pltpu.roll(w, 1, 1), 0.0)
            p2 = jnp.where(lane >= 2, pltpu.roll(w, 2, 1), 0.0)
            n1 = jnp.where(lane < SLAB - 1, pltpu.roll(w, SLAB - 1, 1), 0.0)
            n2 = jnp.where(lane < SLAB - 2, pltpu.roll(w, SLAB - 2, 1), 0.0)
            img = S2 * (p2 + n2) + S1 * (p1 + n1) + mid * w
            f = time_step / k
            w = jnp.concatenate([f * img[Q // 2:], -f * img[:Q // 2]], axis=0)
            acc = acc + w
        outer_ref[ch] = acc

    def order(o, carry):
        factor = factor_of(o)

        @pl.when(o > 0)
        def _():
            send_first(o)

        @pl.when(o == 0)
        def _():
            for k in range(8):
                local_mat(dip_hbm, dc, k, ls.at[8 + k]).wait()
                remote_mat(dip_hbm, dc, k, 0).wait_recv()

        wr(o, ut.at[o, :, ccol], 0)
        both = ut[o]

        def lower_for(zc):
            for x in range(2):
                cols = pl.ds(pl.multiple_of((x * 4 + zc) * ROWS, ROWS), ROWS)
                pt[o, x, zc] = jnp.dot(both, dc[:, cols], preferred_element_type=F32).astype(BF)

        lower_for(zz(2))
        for d in range(2):
            m_far(o, d).start()
        for d in range(4):
            m_own2(o, d).start()
        for x in range(2):
            m_up2(o, x).start()
        for d in range(2):
            lower_for(zz(d))
            m_near(o, d).start()

        def pass_column(d):
            wr(o, uo.at[o, xh, zz(d, -1), hi], 1 + d)
            m_f2(o, d).start()

        def pass_column_down(d):
            for x in range(2):
                m_f2u(o, d, x).start()

        pass_column(0)
        pass_column(1)
        pass_column_down(0)
        pass_column_down(1)
        wr(o, uo.at[o, 1 - xh, z, lo], 4)
        for d in range(3):
            m_f1(o, d).start()
        pass_column(2)
        pass_column_down(2)
        for d in range(2):
            wr(o, rfar.at[o, d], 22 + d)
            rows = slice(d * half, (d + 1) * half)
            for x in range(2):
                pt[o, x, zz(d), rows] = (pt[o, x, zz(d), rows].astype(F32) + rfar[o, d, x].astype(F32)).astype(BF)
            m_both(o, d).start()
        for x in range(2):
            wr(o, uu.at[o, x, z, lo_up], 5 + x)
        for d in range(3):
            m_f3(o, d).start()
        lower_for(z)

        @pl.when(o == 0)
        def _():
            for k in range(8):
                cols = own_cols(k, c)
                hot = chan_ref[0:1, cols] == lax.broadcasted_iota(jnp.int32, (CH, ROWS), 0)
                for j in range(2):
                    g = jnp.where(hot, ghost_ref[j:j + 1, cols], F32(0.0))
                    top = g.astype(BF)
                    hg[768 + j * CH:768 + (j + 1) * CH, k * ROWS:(k + 1) * ROWS] = top
                    hg[816 + j * CH:816 + (j + 1) * CH, k * ROWS:(k + 1) * ROWS] = (g - top.astype(F32)).astype(BF)
            mine = pl.ds(pl.multiple_of(r * ROWS, ROWS), ROWS)
            hot = chan_ref[0:1, mine] == lax.broadcasted_iota(jnp.int32, (Q, ROWS), 0)
            sh[...] = jnp.transpose(jnp.where(hot, 0.5 * surf_ref[0:1, mine], F32(0.0)))
            slp[...] = jnp.zeros_like(slp)
            for k in range(8):
                local_mat(ham_hbm, hg, k, ls.at[16 + k]).wait()
                remote_mat(ham_hbm, hg, k, 1).wait_recv()
            m_edge(0).wait_recv()
            m_edge(1).wait_recv()

        def chans(j, carry):
            outer_channel(o * 6 + j)
            return carry

        lax.fori_loop(0, 6, chans, 0)

        near_cols = pl.ds(pl.multiple_of(xh * (KHALF // 2), KHALF // 2), KHALF // 2)
        far_cols = pl.ds(pl.multiple_of((1 - xh) * (KHALF // 2), KHALF // 2), KHALF // 2)
        for d in range(3):
            wr(o, uo.at[o, xh, zz(d, -1), lo], 34 + d)
        acc[...] = jnp.dot(hg[:, near_cols], uo[o, xh].reshape(KHALF // 2, Q), preferred_element_type=F32)

        for d in range(2):
            wr(o, rz.at[o, d, :, part[1 - d]], 27 + d)
            wr(o, rz.at[o, d, :, part[d]], 32 + d)
        for x in range(2):
            low = pt[o, x, z].astype(F32) + rz[o, 0, x].astype(F32) + rz[o, 1, x].astype(F32)
            rsum[o, x] = low.astype(BF)
            m_lowx(o, x).start()

        def cols_of(x, zc):
            return pl.ds(pl.multiple_of((x * 4 + zc) * ROWS, ROWS), ROWS)

        def add_own(zc):
            acc[...] += jnp.dot(hg[:, cols_of(1 - xh, zc)], uo[o, 1 - xh, zc], preferred_element_type=F32)

        def upper_of(x, zc):
            return jnp.dot(dc[:, cols_of(x, zc)], uu[o, x, zc], preferred_element_type=F32)

        wr(o, uo.at[o, 1 - xh, z, hi], 37)
        add_own(z)
        for x in range(2):
            wr(o, uu.at[o, x, z, hi_up], 38 + x)
        accu[...] = upper_of(0, z) + upper_of(1, z)
        for d in range(3):
            wr(o, uo.at[o, 1 - xh, zz(d, -1), lo], 7 + d)
            wr(o, uo.at[o, 1 - xh, zz(d, -1), hi], 10 + d)
            add_own(zz(d, -1))
        prod = acc[...]
        gpart = prod[768:816] + prod[816:864]
        for j in range(2):
            hp[o, j, 0:ROWS] = prod[j * ROWS:(j + 1) * ROWS]
            hp[o, j, ROWS:ROWS + 48] = gpart
        m_hp(o).start()

        for d in range(3):
            for x in range(2):
                wr(o, uu.at[o, x, zz(d, -1), hi_up], 13 + x * 3 + d)
            wr(o, uu.at[o, :, zz(d, -1), lo_up], 19 + d)
            accu[...] += upper_of(0, zz(d, -1)) + upper_of(1, zz(d, -1))
        prod = accu[...]
        for j in range(2):
            up[o, j] = prod[j * ROWS:(j + 1) * ROWS]
        m_upp(o).start()

        wr(o, hr.at[o], 30)
        ghs[...] = hr[o, ROWS:ROWS + 48] + hp[o, c, ROWS:ROWS + 48]
        ghost0 = ghs[0:CH]
        ghost1 = ghs[CH:2 * CH]

        @pl.when((o == 0) & (r != 0))
        def _():
            m_first(1).wait_recv()

        slp[0:CH] = (ab[o] + cs[3] - ghost0) * (1.0 / (2.0 * spacing))
        source = jnp.dot(sh[...], slp[...], precision=lax.Precision.HIGHEST, preferred_element_type=F32)
        first = r == 0
        last = r == 15
        dl[0] = jnp.where(first, ghost1, tl[6])
        dl[1] = jnp.where(first, ghost0, tl[7])
        dr[10] = jnp.where(last, 0.0, tr[8])
        dr[11] = jnp.where(last, 0.0, tr[9])
        cs[0] = ghost1
        cs[1] = ghost0

        def advance(ref, first_index, count, inv):
            out = [
                factor * spin(image(ref[i - 2], ref[i - 1], ref[i], ref[i + 1], ref[i + 2], inv(i)))
                for i in range(first_index, first_index + count)
            ]
            for i in range(count):
                ref[first_index + i] = out[i]

        advance(tl, 2, 12, lambda i: invr[i:i + 1, :])
        advance(tr, 2, 12, lambda i: invr[16 + i:17 + i, :])
        advance(dl, 2, 8, lambda i: invr[6 + i:7 + i, :])
        advance(dr, 2, 8, lambda i: invr[14 + i:15 + i, :])
        advance(cs, 2, 8, lambda i: inv_first(i - 2))
        ct[0:8] = ct[0:8] + dl[2:10]
        ct[8:16] = ct[8:16] + dr[2:10]

        @pl.when(o == TERMS - 1)
        def _():
            for p in range(16):
                pack[packed(p), :] = ct[p]

            def fix(g, carry):
                block = jnp.transpose(pack[pl.ds(pl.multiple_of(g * SLAB, SLAB), SLAB)])
                for j in range(8):
                    turned = pltpu.roll(block, (SLAB - 16 * j - 8) % SLAB, 1)
                    keep = jnp.where((lane < 8) | (lane >= SLAB - 8), turned, 0.0)
                    outer_ref[g * 8 + j] = outer_ref[g * 8 + j] + keep
                return carry

            lax.fori_loop(0, CH // 8, fix, 0)
            pltpu.make_async_copy(outer_ref, outer_out, ls.at[1]).start()

        for x in range(2):
            wr(o, rl.at[o, x], 25 + x)
        low = jnp.transpose(rl[o, 0].astype(F32) + rl[o, 1].astype(F32))
        wr(o, ur.at[o], 31)
        img = (
            hp[o, c, 0:ROWS] + hr[o, 0:ROWS] + source
            + col_upper * (up[o, c] + ur[o])
            + jnp.where(s == 0, 0.0, col_lower * low)
        )
        new = factor * spin(img)
        uf[...] = new
        total_ref[...] = total_ref[...] + new
        return carry

    lax.fori_loop(0, TERMS, order, 0)

    cend = pltpu.make_async_copy(total_ref, total_hbm, ls.at[0])
    cend.start()

    def drain(o, carry):
        for m in all_msgs(o):
            m.wait_send()
        return carry

    lax.fori_loop(0, TERMS, drain, 0)
    for k in range(8):
        remote_mat(dip_hbm, dc, k, 0).wait_send()
        remote_mat(ham_hbm, hg, k, 1).wait_send()
    m_edge(0).wait_send()
    m_edge(1).wait_send()
    pltpu.make_async_copy(outer_ref, outer_out, ls.at[1]).wait()
    cend.wait()

    @pl.when(r == 0)
    def _():
        for j in range(1, 16):
            m_first(j).wait_send()


def finish(total_hbm, outer_hbm, inner_out, outer_out, total, outer, sems):
    pairs = [(total_hbm, total, inner_out)]
    for i in range(3):
        part = pl.ds(i * 8, 8)
        pairs.append((outer_hbm.at[part], outer.at[part], outer_out.at[part]))
    loads = [pltpu.make_async_copy(a, b, sems.at[0, i]) for i, (a, b, _) in enumerate(pairs)]
    stores = [pltpu.make_async_copy(b, c, sems.at[1, i]) for i, (_, b, c) in enumerate(pairs)]
    for copy in loads:
        copy.start()
    for load, store in zip(loads, stores):
        load.wait()
        store.start()
    for copy in stores:
        copy.wait()


def per_device(
    inner_state, outer_state, block_hamiltonian, dipole, field_strength, dipole_links,
    ghost_amplitude, surface_amplitude, state_channel, threshold,
):
    any_ = pl.BlockSpec(memory_space=pl.ANY)
    dma = pltpu.SemaphoreType.DMA
    total, outer = pl.pallas_call(
        kernel,
        out_shape=(
            jax.ShapeDtypeStruct((ROWS, Q), F32),
            jax.ShapeDtypeStruct((CH, Q, SLAB), F32),
        ),
        in_specs=[any_] * 10,
        out_specs=(any_,) * 2,
        scratch_shapes=[
            pltpu.VMEM((1, Q // 2), F32),
            pltpu.VMEM((7, Q // 2), jnp.int32),
            pltpu.VMEM((1, CH), F32),
            pltpu.VMEM((2, STATES), F32),
            pltpu.VMEM((1, STATES), F32),
            pltpu.VMEM((1, STATES), jnp.int32),
            pltpu.VMEM((ROWS, Q), F32),
            pltpu.VMEM((CH, Q, SLAB), F32),
            pltpu.VMEM((16, CH, Q), F32),
            pltpu.VMEM((CH * 16, Q), F32),
            pltpu.VMEM((ROWS, Q), F32),
            pltpu.VMEM((TERMS, 2, 4, ROWS, Q), BF),
            pltpu.VMEM((TERMS, 2, 4, ROWS, Q), BF),
            pltpu.VMEM((TERMS, Q, 2 * ROWS), BF),
            pltpu.VMEM((TERMS, 2, 4, Q, ROWS), BF),
            pltpu.VMEM((TERMS, 2, 2, Q // 2, ROWS), BF),
            pltpu.VMEM((TERMS, 2, 2, Q, ROWS), BF),
            pltpu.VMEM((TERMS, 2, Q, ROWS), BF),
            pltpu.VMEM((TERMS, 2, Q, ROWS), BF),
            pltpu.VMEM((864, Q), F32),
            pltpu.VMEM((768, Q), F32),
            pltpu.VMEM((TERMS, 2, ROWS + 48, Q), F32),
            pltpu.VMEM((TERMS, ROWS + 48, Q), F32),
            pltpu.VMEM((TERMS, 2, ROWS, Q), F32),
            pltpu.VMEM((TERMS, ROWS, Q), F32),
            pltpu.VMEM((864, KHALF), BF),
            pltpu.VMEM((768, KHALF), BF),
            pltpu.VMEM((ROWS, Q), F32),
            pltpu.VMEM((Q, Q), F32),
            pltpu.VMEM((16, CH, Q), F32),
            pltpu.VMEM((CH, Q), F32),
            pltpu.VMEM((16, CH, Q), F32),
            pltpu.VMEM((16, CH, Q), F32),
            pltpu.VMEM((12, CH, Q), F32),
            pltpu.VMEM((12, CH, Q), F32),
            pltpu.VMEM((12, CH, Q), F32),
            pltpu.VMEM((TERMS, CH, Q), F32),
            pltpu.VMEM((32, Q), F32),
            pltpu.VMEM((48, Q), F32),
            dma((TERMS, 40)), dma((TERMS, 40)),
            dma((2,)), dma((2,)),
            dma((16,)), dma,
            dma((2, 8)), dma((2, 8)),
            dma((24,)),
        ],
        compiler_params=pltpu.CompilerParams(
            collective_id=0, has_side_effects=True, vmem_limit_bytes=62 * 1024 * 1024
        ),
        name="propagate",
    )(
        inner_state[0], outer_state[0], block_hamiltonian[0], dipole[0], field_strength[None],
        dipole_links, threshold, ghost_amplitude[0], surface_amplitude, state_channel,
    )
    inner_next, outer_next = pl.pallas_call(
        finish,
        out_shape=(
            jax.ShapeDtypeStruct((ROWS, Q), F32),
            jax.ShapeDtypeStruct((CH, Q, SLAB), F32),
        ),
        in_specs=[any_] * 2,
        out_specs=(any_,) * 2,
        scratch_shapes=[pltpu.VMEM((ROWS, Q), F32), pltpu.VMEM((CH, Q, SLAB), F32), dma((2, 4))],
        name="finish",
    )(total, outer)
    return inner_next[None], outer_next[None]


def solution(mesh):
    return jax.shard_map(
        per_device,
        mesh=mesh,
        in_specs=(
            P("sym", "row", None),
            P("sym", None, None, "row"),
            P("sym", "row", None),
            P("sym", "row", None),
            P(),
            P(),
            P("sym", None, None),
            P("sym", None),
            P("sym", None),
            P("sym", None),
        ),
        out_specs=(P("sym", "row", None), P("sym", None, None, "row")),
        check_vma=False,
    )
```

```python
import jax
import jax.numpy as jnp
from jax import lax
from jax.experimental import pallas as pl
from jax.experimental.pallas import tpu as pltpu
from jax.sharding import PartitionSpec as P

TERMS = 4
time_step = 2.0
spacing = 1.5
radius_start = 20.0
charge = 1.0

MESH = pl.DeviceIdType.MESH
BF = jnp.bfloat16
F32 = jnp.float32

ROWS = 384
FIRST = 48
FIRST_UP = 192
STATES = 6144
KHALF = 3072
CH = 24
Q = 128
SLAB = 128
S0 = 15.0 / (12.0 * spacing * spacing)
S1 = -8.0 / (12.0 * spacing * spacing)
S2 = 0.5 / (12.0 * spacing * spacing)


def kernel(
    inner_hbm, outer_hbm, ham_hbm, dip_hbm, *rest,
):
    small_hbm, (total_hbm, outer_out), scratch = rest[:6], rest[6:8], rest[8:]
    small, scratch = scratch[:6], scratch[6:]
    field_ref, link_ref, thr_ref, ghost_ref, surf_ref, chan_ref = small
    (
        total_ref, outer_ref, ct, pack,
        uf, uo, uu, ut, pt, rfar, rz, rsum, rl, acc, accu, hp, hr, up, ur, hg, dc, sh, slp,
        edge_ref, thr_col, tl, tr, dl, dr, cs, ab, invr, ghs,
        ss, rs, es_s, es_r, as_s, as_r, ms_s, ms_r, ls,
    ) = scratch
    s = lax.axis_index("sym")
    r = lax.axis_index("row")
    xh = r // 8
    z = (r // 2) % 4
    c = r % 2
    deltas = (1, 3, 2)

    def zz(d, sign=1):
        return (z + sign * deltas[d] + 4) % 4

    def dev(b, x, zc):
        return (b, x * 8 + zc * 2 + c)

    below = (s + 7) % 8
    above = (s + 1) % 8
    partner = (s, xh * 8 + z * 2 + (1 - c))
    zdev = [dev(s, xh, zz(d)) for d in range(3)]
    xdev = dev(s, 1 - xh, z)

    cin = pltpu.make_async_copy(inner_hbm, uf, ls.at[0])
    cin.start()
    csmall = [pltpu.make_async_copy(small_hbm[i], small[i], ls.at[2 + i]) for i in range(6)]
    for copy in csmall:
        copy.start()

    def own_cols(k, core):
        return pl.ds(pl.multiple_of((2 * k + core) * ROWS, ROWS), ROWS)

    crow = pl.ds(pl.multiple_of(c * ROWS, ROWS), ROWS)

    def local_mat(src, dst, k, sem):
        return pltpu.make_async_copy(
            src.at[:, own_cols(k, c)], dst.at[crow, pl.ds(k * ROWS, ROWS)], sem
        )

    def remote_mat(src, dst, k, i):
        return pltpu.make_async_remote_copy(
            src_ref=src.at[:, own_cols(k, 1 - c)], dst_ref=dst.at[crow, pl.ds(k * ROWS, ROWS)],
            send_sem=ms_s.at[i, k], recv_sem=ms_r.at[i, k], device_id=partner, device_id_type=MESH,
        )

    for k in range(8):
        local_mat(dip_hbm, dc, k, ls.at[8 + k]).start()
    cout = pltpu.make_async_copy(outer_hbm, outer_ref, ls.at[1])
    cout.start()

    barrier = pltpu.get_barrier_semaphore()
    for j in range(1, 16):
        pl.semaphore_signal(barrier, inc=1, device_id=(s, (r + j) % 16), device_id_type=MESH)
    for x in range(2):
        pl.semaphore_signal(barrier, inc=1, device_id=dev(above, x, z), device_id_type=MESH)
        pl.semaphore_signal(barrier, inc=1, device_id=dev(below, x, z), device_id_type=MESH)
    pl.semaphore_wait(barrier, 19)

    for k in range(8):
        remote_mat(dip_hbm, dc, k, 0).start()

    def rc(o, src, dst, si, ri, device):
        return pltpu.make_async_remote_copy(
            src_ref=src, dst_ref=dst, send_sem=ss.at[o, si], recv_sem=rs.at[o, ri],
            device_id=device, device_id_type=MESH,
        )

    lo = pl.ds(0, FIRST)
    hi = pl.ds(FIRST, ROWS - FIRST)
    lo_up = pl.ds(0, FIRST_UP)
    hi_up = pl.ds(FIRST_UP, ROWS - FIRST_UP)
    ccol = pl.ds(pl.multiple_of(c * ROWS, ROWS), ROWS)

    def m_core(o):
        return rc(o, ut.at[o, :, ccol], ut.at[o, :, ccol], 0, 0, partner)

    def m_own(o, d):
        ref = uo.at[o, xh, z, hi if d < 3 else lo]
        return rc(o, ref, ref, 1 + d, 1 + d, zdev[d] if d < 3 else xdev)

    def m_own2(o, d):
        ref = uo.at[o, xh, z, lo if d < 3 else hi]
        return rc(o, ref, ref, 34 + d, 34 + d, zdev[d] if d < 3 else xdev)

    def m_up(o, x):
        return rc(o, uo.at[o, xh, z, lo_up], uu.at[o, xh, z, lo_up], 5 + x, 5 + xh, dev(below, x, z))

    def m_up2(o, x):
        return rc(o, uo.at[o, xh, z, hi_up], uu.at[o, xh, z, hi_up], 38 + x, 38 + xh, dev(below, x, z))

    def m_f1(o, d):
        ref = uo.at[o, 1 - xh, z, lo]
        return rc(o, ref, ref, 7 + d, 7 + d, zdev[d])

    def m_f2(o, d):
        ref = uo.at[o, xh, zz(d, -1), hi]
        return rc(o, ref, ref, 10 + d, 10 + d, xdev)

    def m_f2u(o, d, x):
        return rc(o, uo.at[o, xh, zz(d, -1), hi_up], uu.at[o, xh, zz(d, -1), hi_up],
                  13 + x * 3 + d, 13 + xh * 3 + d, dev(below, x, z))

    def m_f3(o, d):
        ref = uu.at[o, :, z, lo_up]
        return rc(o, ref, ref, 19 + d, 19 + d, zdev[d])

    half = Q // 2
    part = (pl.ds(0, half), pl.ds(half, half))

    def m_far(o, d):
        return rc(o, pt.at[o, :, zz(2), part[d]], rfar.at[o, d], 22 + d, 22 + d, zdev[d])

    def m_near(o, d):
        return rc(o, pt.at[o, :, zz(d), part[1 - d]], rz.at[o, d, :, part[1 - d]], 27 + d, 27 + d, zdev[d])

    def m_both(o, d):
        return rc(o, pt.at[o, :, zz(d), part[d]], rz.at[o, d, :, part[d]], 32 + d, 32 + d, zdev[d])

    def m_lowx(o, x):
        return rc(o, rsum.at[o, x], rl.at[o, xh], 25 + x, 25 + xh, dev(above, x, z))

    def m_hp(o):
        return rc(o, hp.at[o, 1 - c], hr.at[o], 30, 30, partner)

    def m_upp(o):
        return rc(o, up.at[o, 1 - c], ur.at[o], 31, 31, partner)

    def wr(o, dst, ri):
        rc(o, dst, dst, ri, ri, partner).wait_recv()

    def all_msgs(o):
        out = [m_core(o)]
        out += [m(o, d) for d in range(4) for m in (m_own, m_own2)]
        out += [m(o, x) for x in range(2) for m in (m_up, m_up2)]
        out += [m_f1(o, d) for d in range(3)] + [m_f2(o, d) for d in range(3)]
        out += [m_f2u(o, d, x) for x in range(2) for d in range(3)]
        out += [m_f3(o, d) for d in range(3)]
        out += [m(o, d) for d in range(2) for m in (m_far, m_near, m_both, m_lowx)]
        return out + [m_hp(o), m_upp(o)]

    right = (s, (r + 1) % 16)
    left = (s, (r + 15) % 16)

    def m_edge(i):
        src = edge_ref.at[pl.ds(8, 8)] if i == 0 else edge_ref.at[pl.ds(0, 8)]
        dst = tl.at[pl.ds(0, 8)] if i == 0 else tr.at[pl.ds(8, 8)]
        return pltpu.make_async_remote_copy(
            src_ref=src, dst_ref=dst, send_sem=es_s.at[i], recv_sem=es_r.at[i],
            device_id=right if i == 0 else left, device_id_type=MESH,
        )

    def m_first(j):
        return pltpu.make_async_remote_copy(
            src_ref=ab, dst_ref=ab, send_sem=as_s.at[j], recv_sem=as_r,
            device_id=(s, j), device_id_type=MESH,
        )

    lane = lax.broadcasted_iota(jnp.int32, (1, Q), 1)
    sign = jnp.where(lane < Q // 2, F32(1.0), F32(-1.0))

    def spin(x):
        return pltpu.roll(x, Q // 2, 1) * sign

    cin.wait()

    for copy in csmall:
        copy.wait()
    pos = lax.broadcasted_iota(jnp.int32, (32, Q), 0)
    pos = jnp.where(pos < 16, pos - 8, pos + 104) + r * SLAB
    invr[...] = charge / (radius_start + spacing * pos.astype(F32))
    square = (CH, CH)
    eye = lax.broadcasted_iota(jnp.int32, square, 0) == lax.broadcasted_iota(jnp.int32, square, 1)
    column = jnp.sum(jnp.where(eye, jnp.broadcast_to(thr_ref[0:1, :], square), 0.0), axis=1, keepdims=True)
    thr_col[...] = jnp.broadcast_to(column, (CH, Q))
    thr = thr_col[...]

    def image(two_low, low, mid, high, two_high, inv):
        return S2 * (two_low + two_high) + S1 * (low + high) + (S0 + thr - inv) * mid

    def inv_first(p):
        return charge / (radius_start + spacing * p)

    def factor_of(o):
        return jnp.where(o == 0, F32(2.0), jnp.where(o == 1, F32(1.0), jnp.where(o == 2, F32(2.0 / 3.0), F32(0.5))))

    total_ref[...] = uf[...]

    def send_first(o):
        u = uf[...]
        uo[o, xh, z] = u.astype(BF)
        for d in range(4):
            m_own(o, d).start()
        for x in range(2):
            m_up(o, x).start()
        ut[o, :, ccol] = jnp.transpose(u).astype(BF)
        m_core(o).start()

    send_first(0)
    for k in range(8):
        local_mat(ham_hbm, hg, k, ls.at[16 + k]).start()
        remote_mat(ham_hbm, hg, k, 1).start()
    cout.wait()

    def edges(g, carry):
        block = jnp.zeros((Q, SLAB), F32)
        for j in range(8):
            turned = pltpu.roll(outer_ref[g * 8 + j], (16 * j + 8) % SLAB, 1)
            block = jnp.where((lane >= 16 * j) & (lane < 16 * j + 16), turned, block)
        pack[pl.ds(pl.multiple_of(g * SLAB, SLAB), SLAB)] = jnp.transpose(block)
        return carry

    lax.fori_loop(0, CH // 8, edges, 0)

    def packed(p):
        return pl.ds((p + 8) % 16, CH, stride=16)

    for p in range(16):
        edge_ref[p] = pack[packed(p), :]
    m_edge(0).start()
    m_edge(1).start()

    @pl.when(r == 0)
    def _():
        zero = jnp.zeros((CH, Q), F32)
        strip = [edge_ref[p] for p in range(8)]
        ab[0] = strip[1]
        for k in range(1, TERMS):
            keep = 8 - 2 * k
            ext = [zero, zero] + strip
            strip = [
                (time_step / k) * spin(image(ext[p], ext[p + 1], ext[p + 2], ext[p + 3], ext[p + 4], inv_first(p)))
                for p in range(keep)
            ]
            ab[k] = strip[1]
        for j in range(1, 16):
            m_first(j).start()

    for ref in (dl, dr, cs, ct):
        ref[...] = jnp.zeros_like(ref)
    tl[8:16] = edge_ref[0:8]
    tr[0:8] = edge_ref[8:16]

    def doubled(x):
        return jnp.concatenate([x, x], axis=1)

    def coupled_field(b):
        row = link_ref[pl.ds(jnp.clip(b, 0, 6), 1), :].astype(F32) * field_ref[...]
        return doubled(jnp.where((b >= 0) & (b < 7), row, 0.0))

    col_upper = coupled_field(s)
    col_lower = coupled_field(s - 1)
    pos_lane = (lax.broadcasted_iota(jnp.int32, (1, SLAB), 1) + r * SLAB).astype(F32)
    lane_inv = charge / (radius_start + spacing * pos_lane)

    def outer_channel(ch):
        w = outer_ref[ch]
        acc = w
        mid = (S0 + thr_col[pl.ds(ch, 1), :]) - lane_inv
        for k in range(1, TERMS + 1):
            p1 = jnp.where(lane >= 1, pltpu.roll(w, 1, 1), 0.0)
            p2 = jnp.where(lane >= 2, pltpu.roll(w, 2, 1), 0.0)
            n1 = jnp.where(lane < SLAB - 1, pltpu.roll(w, SLAB - 1, 1), 0.0)
            n2 = jnp.where(lane < SLAB - 2, pltpu.roll(w, SLAB - 2, 1), 0.0)
            img = S2 * (p2 + n2) + S1 * (p1 + n1) + mid * w
            f = time_step / k
            w = jnp.concatenate([f * img[Q // 2:], -f * img[:Q // 2]], axis=0)
            acc = acc + w
        outer_ref[ch] = acc

    def order(o, carry):
        factor = factor_of(o)

        @pl.when(o > 0)
        def _():
            send_first(o)

        @pl.when(o == 0)
        def _():
            for k in range(8):
                local_mat(dip_hbm, dc, k, ls.at[8 + k]).wait()
                remote_mat(dip_hbm, dc, k, 0).wait_recv()

        wr(o, ut.at[o, :, ccol], 0)
        both = ut[o]

        def lower_for(zc):
            for x in range(2):
                cols = pl.ds(pl.multiple_of((x * 4 + zc) * ROWS, ROWS), ROWS)
                pt[o, x, zc] = jnp.dot(both, dc[:, cols], preferred_element_type=F32).astype(BF)

        lower_for(zz(2))
        for d in range(2):
            m_far(o, d).start()
        for d in range(4):
            m_own2(o, d).start()
        for x in range(2):
            m_up2(o, x).start()
        for d in range(2):
            lower_for(zz(d))
            m_near(o, d).start()

        def pass_column(d):
            wr(o, uo.at[o, xh, zz(d, -1), hi], 1 + d)
            m_f2(o, d).start()

        def pass_column_down(d):
            for x in range(2):
                m_f2u(o, d, x).start()

        pass_column(0)
        pass_column(1)
        pass_column_down(0)
        pass_column_down(1)
        pass_column(2)
        pass_column_down(2)
        for d in range(2):
            wr(o, rfar.at[o, d], 22 + d)
            rows = slice(d * half, (d + 1) * half)
            for x in range(2):
                pt[o, x, zz(d), rows] = (pt[o, x, zz(d), rows].astype(F32) + rfar[o, d, x].astype(F32)).astype(BF)
            m_both(o, d).start()
        wr(o, uo.at[o, 1 - xh, z, lo], 4)
        for d in range(3):
            m_f1(o, d).start()
        for x in range(2):
            wr(o, uu.at[o, x, z, lo_up], 5 + x)
        for d in range(3):
            m_f3(o, d).start()
        lower_for(z)

        @pl.when(o == 0)
        def _():
            for k in range(8):
                cols = own_cols(k, c)
                hot = chan_ref[0:1, cols] == lax.broadcasted_iota(jnp.int32, (CH, ROWS), 0)
                for j in range(2):
                    g = jnp.where(hot, ghost_ref[j:j + 1, cols], F32(0.0))
                    top = g.astype(BF)
                    hg[768 + j * CH:768 + (j + 1) * CH, k * ROWS:(k + 1) * ROWS] = top
                    hg[816 + j * CH:816 + (j + 1) * CH, k * ROWS:(k + 1) * ROWS] = (g - top.astype(F32)).astype(BF)
            mine = pl.ds(pl.multiple_of(r * ROWS, ROWS), ROWS)
            hot = chan_ref[0:1, mine] == lax.broadcasted_iota(jnp.int32, (Q, ROWS), 0)
            sh[...] = jnp.transpose(jnp.where(hot, 0.5 * surf_ref[0:1, mine], F32(0.0)))
            slp[...] = jnp.zeros_like(slp)
            for k in range(8):
                local_mat(ham_hbm, hg, k, ls.at[16 + k]).wait()
                remote_mat(ham_hbm, hg, k, 1).wait_recv()
            m_edge(0).wait_recv()
            m_edge(1).wait_recv()

        def chans(j, carry):
            outer_channel(o * 6 + j)
            return carry

        lax.fori_loop(0, 6, chans, 0)

        near_cols = pl.ds(pl.multiple_of(xh * (KHALF // 2), KHALF // 2), KHALF // 2)
        far_cols = pl.ds(pl.multiple_of((1 - xh) * (KHALF // 2), KHALF // 2), KHALF // 2)
        for d in range(3):
            wr(o, uo.at[o, xh, zz(d, -1), lo], 34 + d)
        acc[...] = jnp.dot(hg[:, near_cols], uo[o, xh].reshape(KHALF // 2, Q), preferred_element_type=F32)

        for d in range(2):
            wr(o, rz.at[o, d, :, part[1 - d]], 27 + d)
            wr(o, rz.at[o, d, :, part[d]], 32 + d)
        for x in range(2):
            low = pt[o, x, z].astype(F32) + rz[o, 0, x].astype(F32) + rz[o, 1, x].astype(F32)
            rsum[o, x] = low.astype(BF)
            m_lowx(o, x).start()

        def cols_of(x, zc):
            return pl.ds(pl.multiple_of((x * 4 + zc) * ROWS, ROWS), ROWS)

        def add_own(zc):
            acc[...] += jnp.dot(hg[:, cols_of(1 - xh, zc)], uo[o, 1 - xh, zc], preferred_element_type=F32)

        def upper_of(x, zc):
            return jnp.dot(dc[:, cols_of(x, zc)], uu[o, x, zc], preferred_element_type=F32)

        wr(o, uo.at[o, 1 - xh, z, hi], 37)
        add_own(z)
        for x in range(2):
            wr(o, uu.at[o, x, z, hi_up], 38 + x)
        accu[...] = upper_of(0, z) + upper_of(1, z)
        for d in range(3):
            wr(o, uo.at[o, 1 - xh, zz(d, -1), lo], 7 + d)
            wr(o, uo.at[o, 1 - xh, zz(d, -1), hi], 10 + d)
            add_own(zz(d, -1))
        prod = acc[...]
        gpart = prod[768:816] + prod[816:864]
        for j in range(2):
            hp[o, j, 0:ROWS] = prod[j * ROWS:(j + 1) * ROWS]
            hp[o, j, ROWS:ROWS + 48] = gpart
        m_hp(o).start()

        for d in range(3):
            for x in range(2):
                wr(o, uu.at[o, x, zz(d, -1), hi_up], 13 + x * 3 + d)
            wr(o, uu.at[o, :, zz(d, -1), lo_up], 19 + d)
            accu[...] += upper_of(0, zz(d, -1)) + upper_of(1, zz(d, -1))
        prod = accu[...]
        for j in range(2):
            up[o, j] = prod[j * ROWS:(j + 1) * ROWS]
        m_upp(o).start()

        wr(o, hr.at[o], 30)
        ghs[...] = hr[o, ROWS:ROWS + 48] + hp[o, c, ROWS:ROWS + 48]
        ghost0 = ghs[0:CH]
        ghost1 = ghs[CH:2 * CH]

        @pl.when((o == 0) & (r != 0))
        def _():
            m_first(1).wait_recv()

        slp[0:CH] = (ab[o] + cs[3] - ghost0) * (1.0 / (2.0 * spacing))
        source = jnp.dot(sh[...], slp[...], precision=lax.Precision.HIGHEST, preferred_element_type=F32)
        first = r == 0
        last = r == 15
        dl[0] = jnp.where(first, ghost1, tl[6])
        dl[1] = jnp.where(first, ghost0, tl[7])
        dr[10] = jnp.where(last, 0.0, tr[8])
        dr[11] = jnp.where(last, 0.0, tr[9])
        cs[0] = ghost1
        cs[1] = ghost0

        def advance(ref, first_index, count, inv):
            out = [
                factor * spin(image(ref[i - 2], ref[i - 1], ref[i], ref[i + 1], ref[i + 2], inv(i)))
                for i in range(first_index, first_index + count)
            ]
            for i in range(count):
                ref[first_index + i] = out[i]

        advance(tl, 2, 12, lambda i: invr[i:i + 1, :])
        advance(tr, 2, 12, lambda i: invr[16 + i:17 + i, :])
        advance(dl, 2, 8, lambda i: invr[6 + i:7 + i, :])
        advance(dr, 2, 8, lambda i: invr[14 + i:15 + i, :])
        advance(cs, 2, 8, lambda i: inv_first(i - 2))
        ct[0:8] = ct[0:8] + dl[2:10]
        ct[8:16] = ct[8:16] + dr[2:10]

        @pl.when(o == TERMS - 1)
        def _():
            for p in range(16):
                pack[packed(p), :] = ct[p]

            def fix(g, carry):
                block = jnp.transpose(pack[pl.ds(pl.multiple_of(g * SLAB, SLAB), SLAB)])
                for j in range(8):
                    turned = pltpu.roll(block, (SLAB - 16 * j - 8) % SLAB, 1)
                    keep = jnp.where((lane < 8) | (lane >= SLAB - 8), turned, 0.0)
                    outer_ref[g * 8 + j] = outer_ref[g * 8 + j] + keep
                return carry

            lax.fori_loop(0, CH // 8, fix, 0)
            pltpu.make_async_copy(outer_ref, outer_out, ls.at[1]).start()

        for x in range(2):
            wr(o, rl.at[o, x], 25 + x)
        low = jnp.transpose(rl[o, 0].astype(F32) + rl[o, 1].astype(F32))
        wr(o, ur.at[o], 31)
        img = (
            hp[o, c, 0:ROWS] + hr[o, 0:ROWS] + source
            + col_upper * (up[o, c] + ur[o])
            + jnp.where(s == 0, 0.0, col_lower * low)
        )
        new = factor * spin(img)
        uf[...] = new
        total_ref[...] = total_ref[...] + new
        return carry

    lax.fori_loop(0, TERMS, order, 0)

    cend = pltpu.make_async_copy(total_ref, total_hbm, ls.at[0])
    cend.start()

    def drain(o, carry):
        for m in all_msgs(o):
            m.wait_send()
        return carry

    lax.fori_loop(0, TERMS, drain, 0)
    for k in range(8):
        remote_mat(dip_hbm, dc, k, 0).wait_send()
        remote_mat(ham_hbm, hg, k, 1).wait_send()
    m_edge(0).wait_send()
    m_edge(1).wait_send()
    pltpu.make_async_copy(outer_ref, outer_out, ls.at[1]).wait()
    cend.wait()

    @pl.when(r == 0)
    def _():
        for j in range(1, 16):
            m_first(j).wait_send()


def finish(total_hbm, outer_hbm, inner_out, outer_out, total, outer, sems):
    pairs = [(total_hbm, total, inner_out)]
    for i in range(3):
        part = pl.ds(i * 8, 8)
        pairs.append((outer_hbm.at[part], outer.at[part], outer_out.at[part]))
    loads = [pltpu.make_async_copy(a, b, sems.at[0, i]) for i, (a, b, _) in enumerate(pairs)]
    stores = [pltpu.make_async_copy(b, c, sems.at[1, i]) for i, (_, b, c) in enumerate(pairs)]
    for copy in loads:
        copy.start()
    for load, store in zip(loads, stores):
        load.wait()
        store.start()
    for copy in stores:
        copy.wait()


def per_device(
    inner_state, outer_state, block_hamiltonian, dipole, field_strength, dipole_links,
    ghost_amplitude, surface_amplitude, state_channel, threshold,
):
    any_ = pl.BlockSpec(memory_space=pl.ANY)
    dma = pltpu.SemaphoreType.DMA
    total, outer = pl.pallas_call(
        kernel,
        out_shape=(
            jax.ShapeDtypeStruct((ROWS, Q), F32),
            jax.ShapeDtypeStruct((CH, Q, SLAB), F32),
        ),
        in_specs=[any_] * 10,
        out_specs=(any_,) * 2,
        scratch_shapes=[
            pltpu.VMEM((1, Q // 2), F32),
            pltpu.VMEM((7, Q // 2), jnp.int32),
            pltpu.VMEM((1, CH), F32),
            pltpu.VMEM((2, STATES), F32),
            pltpu.VMEM((1, STATES), F32),
            pltpu.VMEM((1, STATES), jnp.int32),
            pltpu.VMEM((ROWS, Q), F32),
            pltpu.VMEM((CH, Q, SLAB), F32),
            pltpu.VMEM((16, CH, Q), F32),
            pltpu.VMEM((CH * 16, Q), F32),
            pltpu.VMEM((ROWS, Q), F32),
            pltpu.VMEM((TERMS, 2, 4, ROWS, Q), BF),
            pltpu.VMEM((TERMS, 2, 4, ROWS, Q), BF),
            pltpu.VMEM((TERMS, Q, 2 * ROWS), BF),
            pltpu.VMEM((TERMS, 2, 4, Q, ROWS), BF),
            pltpu.VMEM((TERMS, 2, 2, Q // 2, ROWS), BF),
            pltpu.VMEM((TERMS, 2, 2, Q, ROWS), BF),
            pltpu.VMEM((TERMS, 2, Q, ROWS), BF),
            pltpu.VMEM((TERMS, 2, Q, ROWS), BF),
            pltpu.VMEM((864, Q), F32),
            pltpu.VMEM((768, Q), F32),
            pltpu.VMEM((TERMS, 2, ROWS + 48, Q), F32),
            pltpu.VMEM((TERMS, ROWS + 48, Q), F32),
            pltpu.VMEM((TERMS, 2, ROWS, Q), F32),
            pltpu.VMEM((TERMS, ROWS, Q), F32),
            pltpu.VMEM((864, KHALF), BF),
            pltpu.VMEM((768, KHALF), BF),
            pltpu.VMEM((ROWS, Q), F32),
            pltpu.VMEM((Q, Q), F32),
            pltpu.VMEM((16, CH, Q), F32),
            pltpu.VMEM((CH, Q), F32),
            pltpu.VMEM((16, CH, Q), F32),
            pltpu.VMEM((16, CH, Q), F32),
            pltpu.VMEM((12, CH, Q), F32),
            pltpu.VMEM((12, CH, Q), F32),
            pltpu.VMEM((12, CH, Q), F32),
            pltpu.VMEM((TERMS, CH, Q), F32),
            pltpu.VMEM((32, Q), F32),
            pltpu.VMEM((48, Q), F32),
            dma((TERMS, 40)), dma((TERMS, 40)),
            dma((2,)), dma((2,)),
            dma((16,)), dma,
            dma((2, 8)), dma((2, 8)),
            dma((24,)),
        ],
        compiler_params=pltpu.CompilerParams(
            collective_id=0, has_side_effects=True, vmem_limit_bytes=62 * 1024 * 1024
        ),
        name="propagate",
    )(
        inner_state[0], outer_state[0], block_hamiltonian[0], dipole[0], field_strength[None],
        dipole_links, threshold, ghost_amplitude[0], surface_amplitude, state_channel,
    )
    inner_next, outer_next = pl.pallas_call(
        finish,
        out_shape=(
            jax.ShapeDtypeStruct((ROWS, Q), F32),
            jax.ShapeDtypeStruct((CH, Q, SLAB), F32),
        ),
        in_specs=[any_] * 2,
        out_specs=(any_,) * 2,
        scratch_shapes=[pltpu.VMEM((ROWS, Q), F32), pltpu.VMEM((CH, Q, SLAB), F32), dma((2, 4))],
        name="finish",
    )(total, outer)
    return inner_next[None], outer_next[None]


def solution(mesh):
    return jax.shard_map(
        per_device,
        mesh=mesh,
        in_specs=(
            P("sym", "row", None),
            P("sym", None, None, "row"),
            P("sym", "row", None),
            P("sym", "row", None),
            P(),
            P(),
            P("sym", None, None),
            P("sym", None),
            P("sym", None),
            P("sym", None),
        ),
        out_specs=(P("sym", "row", None), P("sym", None, None, "row")),
        check_vma=False,
    )
```
